128 devices in a mesh: dp: 32 (over x, y, core), tensor: 4 (over z).
Axes of the slice: x: 4, y: 4, z: 4, core: 2. Of those that a mesh axis runs over, the one named last changes fastest.
Arguments:
- patch_rows: bfloat16 [256, 512, 1280], P('dp', None, 'tensor'), may hold values from -6 to 6
- out_grads: bfloat16 [256, 512, 1280], P('dp', None, 'tensor'), may hold values from -0.29882812 to 0.29882812
- basis_a: bfloat16 [27, 1280, 128], P(None, 'tensor', 'dp'), may hold values from -0.03125 to 0.03125
- basis_g: bfloat16 [1280, 1280], P('tensor', 'dp'), may hold values from -0.15625 to 0.15625
Outputs:
- corrections: float32 [128, 1280], P(('dp', 'tensor'))
The draws below stay inside these ranges and needn't reach their ends.
All inputs are finite; a program needn't handle non-finite values.
Results may differ from the reference program's by a relative error of at most 0.00054.
Values may be sent and summed in bfloat16 or wider, within the bound.
No kernel may reach another device: no remote copies, remote signals or barrier semaphores. Data moves between devices by JAX's collectives and lax.ppermute only.
A program may use at most 256 MiB of HBM per device.

```python
import jax
import jax.numpy as jnp
from jax import lax

CIN = 1280
COUT = 1280
SIDE = 8
RANKS = 128
EXAMPLES = 256


def level_of(key, dims, split, smallest, high):
    def one(position, blocks):
        draws = jax.random.uniform(jax.random.fold_in(jax.random.fold_in(key, 6), position), (blocks,), jnp.float32, smallest / len(split), high / len(split))
        return jnp.repeat(jnp.exp(draws), dims[position] // blocks).reshape((-1,) + (1,) * (len(dims) - position - 1))

    gain = one(*split[0])
    for cut in split[1:]:
        gain = gain * one(*cut)
    return gain


def centred(own_key, extent, width, limit, split=(), held_as=jnp.bfloat16):
    loudness = level_of(own_key, extent, split, -0.22, 0.18) if split else 1.0
    entries = jax.random.normal(own_key, extent, jnp.float32) * width * loudness
    return jnp.minimum(jnp.maximum(entries, -limit), limit).astype(held_as)


def setup_inputs(seed: int = 0) -> dict:
    seeds = jax.random.split(jax.random.key(seed), 5)
    patch_rows = centred(seeds[0], (EXAMPLES, SIDE**3, CIN), 1.0, 6.0, ((0, 32), (2, 4)))
    out_grads = centred(seeds[1], (EXAMPLES, SIDE**3, COUT), 0.044, 0.29882812, ((0, 32), (2, 4)))
    basis_a = centred(seeds[2], (27, CIN, RANKS), (27 * CIN) ** -0.5, 0.03125, ((1, 4), (2, 32)))
    basis_g = centred(seeds[3], (COUT, COUT), COUT ** -0.5, 0.15625, ((0, 4), (1, 32)))
    return {"patch_rows": patch_rows, "out_grads": out_grads, "basis_a": basis_a, "basis_g": basis_g}


def padded_grid(rows):
    examples_here = rows.shape[0]
    channels = rows.shape[2]
    volume = rows.reshape(examples_here, SIDE, SIDE, SIDE, channels)
    return jnp.pad(volume, ((0, 0), (1, 1), (1, 1), (1, 1), (0, 0)))


def project_taps(padded, basis, examples_here, channels):
    summed = None
    for offset_x in range(3):
        for offset_y in range(3):
            for offset_z in range(3):
                tap_index = offset_x * 9 + offset_y * 3 + offset_z
                window = padded[:, offset_x:offset_x + SIDE, offset_y:offset_y + SIDE, offset_z:offset_z + SIDE, :]
                window = window.reshape(examples_here * SIDE * SIDE * SIDE, channels)
                tap_term = jnp.dot(window, basis[tap_index], preferred_element_type=jnp.float32)
                summed = tap_term if summed is None else summed + tap_term
    return summed


def reference(patch_rows, out_grads, basis_a, basis_g):
    def accumulate(carry, example_pair):
        rows_one, grads_one = example_pair
        padded = padded_grid(rows_one[None])
        coeff_a = project_taps(padded, basis_a, 1, rows_one.shape[1]).astype(jnp.bfloat16)
        coeff_g = jnp.dot(grads_one, basis_g, preferred_element_type=jnp.float32).astype(jnp.bfloat16)
        products = jnp.dot(coeff_a.T, coeff_g, preferred_element_type=jnp.float32)
        return carry + products * products, None

    initial = jnp.zeros((RANKS, COUT), jnp.float32)
    summed, unused = lax.scan(accumulate, initial, (patch_rows, out_grads))
    return summed / EXAMPLES
```

```python
import functools

import jax
import jax.numpy as jnp
from jax import lax
from jax.experimental import pallas as pl
from jax.experimental.pallas import tpu as pltpu
from jax.sharding import Mesh, PartitionSpec as P

SIDE = 8
POS = SIDE * SIDE * SIDE
AB = 9
HALF = 512
CHIPS = ("x", "y")
ALL = ("x", "y", "core", "z")


def lane_coords():
    p = lax.broadcasted_iota(jnp.int32, (1, POS), 1)
    return p // 64, (p // 8) % 8, p % 8


def shifted(y, ab, i, j):
    a, b = ab // 3 - 1, ab % 3 - 1
    s = a * 64 + b * 8
    if s == 0:
        return y
    ok = None
    for v, o in ((i, a), (j, b)):
        if o != 0:
            m = (v + o >= 0) & (v + o < SIDE)
            ok = m if ok is None else ok & m
    return jnp.where(ok, pltpu.roll(y, (-s) % POS, 1), 0.0)


def conv_kernel(idx_ref, b_own_ref, b_oth_ref, x_ref, o_ref, xc_ref, *, per):
    i, j, k = lane_coords()
    core = idx_ref[0]
    block = idx_ref[1]
    h = x_ref.shape[1]
    b = jnp.concatenate([b_own_ref[...], b_oth_ref[...]], axis=1)

    def put(row, v):
        at = pl.multiple_of((row + core * HALF) % (2 * HALF), 64)
        xc_ref[pl.ds(at, v.shape[0]), :] = v

    for n in range(per):
        x = x_ref[block * per + n]
        xf = x.astype(jnp.float32)
        before = jnp.where(k >= 1, pltpu.roll(xf, 1, 1), 0.0).astype(x.dtype)
        after = jnp.where(k <= SIDE - 2, pltpu.roll(xf, POS - 1, 1), 0.0).astype(x.dtype)
        put(0, before)
        put(h, x[: HALF - h])
        put(HALF, x[HALF - h :])
        put(2 * h, after)
        put(3 * h, jnp.zeros((2 * HALF - 3 * h, POS), x.dtype))
        y = jnp.dot(b, xc_ref[...], preferred_element_type=jnp.float32)
        y = y.reshape(y.shape[0] // (8 * AB), AB, 8, POS)
        acc = None
        for ab in range(AB):
            t = shifted(y[:, ab].reshape(-1, POS), ab, i, j)
            acc = t if acc is None else acc + t
        o_ref[n] = acc.astype(o_ref.dtype)


def conv(idx, b_own, b_oth, x, per, dtype):
    ranks = b_own.shape[0] // AB
    return pl.pallas_call(
        functools.partial(conv_kernel, per=per),
        out_shape=jax.ShapeDtypeStruct((per, ranks, POS), dtype),
        in_specs=[pl.BlockSpec(memory_space=pltpu.SMEM)] + [pl.BlockSpec(memory_space=pltpu.VMEM)] * 3,
        out_specs=pl.BlockSpec(memory_space=pltpu.VMEM),
        scratch_shapes=[pltpu.VMEM((2 * HALF, POS), jnp.bfloat16)],
        compiler_params=pltpu.CompilerParams(vmem_limit_bytes=40 << 20),
        name="conv_taps",
    )(idx, b_own, b_oth, x)


NT = (((1,), (1,)), ((), ()))


def squares_kernel(own_ref, r1_ref, r2_ref, r3_ref, g_ref, bg_ref, o_ref, *, scale):
    per, ranks = own_ref.shape[0], own_ref.shape[1]
    tensor = bg_ref.shape[1]
    total = None
    for n in range(per):
        c = own_ref[n] + r1_ref[n].astype(jnp.float32) + r2_ref[n].astype(jnp.float32) + r3_ref[n].astype(jnp.float32)
        hi = c.astype(jnp.bfloat16)
        lo = (c - hi.astype(jnp.float32)).astype(jnp.bfloat16)
        both = jnp.concatenate([hi, lo], axis=0)
        prod = None
        for z in range(tensor):
            m = lax.dot_general(both, g_ref[z * per + n], NT, preferred_element_type=jnp.float32)
            m = (m[:ranks] + m[ranks:]).astype(jnp.bfloat16)
            bg = bg_ref[:, z].reshape(-1, bg_ref.shape[3])
            t = lax.dot_general(m, bg, NT, preferred_element_type=jnp.float32)
            prod = t if prod is None else prod + t
        sq = prod * prod
        total = sq if total is None else total + sq
    o_ref[...] = total * scale


def squares(own, received, grads, bg, scale):
    return pl.pallas_call(
        functools.partial(squares_kernel, scale=scale),
        out_shape=jax.ShapeDtypeStruct((own.shape[1], bg.shape[0] * bg.shape[2]), jnp.float32),
        in_specs=[pl.BlockSpec(memory_space=pltpu.VMEM)] * 6,
        out_specs=pl.BlockSpec(memory_space=pltpu.VMEM),
        compiler_params=pltpu.CompilerParams(vmem_limit_bytes=40 << 20),
        name="squared_sums",
    )(own, *received, grads, bg)


def shift(v, axis, s):
    n = lax.axis_size(axis)
    return lax.ppermute(v, axis, [(i, (i + s) % n) for i in range(n)])


def body(patch_rows, out_grads, basis_a, basis_g):
    core, z = lax.axis_index("core"), lax.axis_index("z")
    x = patch_rows.transpose(0, 2, 1)
    grads = out_grads.transpose(0, 2, 1)
    here, channels = x.shape[0], x.shape[1]
    tensor = lax.axis_size("z")
    per = here // tensor
    chips = lax.axis_size(CHIPS)

    with jax.named_scope("gather_basis_a"):
        own = basis_a.reshape(AB, 3, channels, -1).transpose(0, 3, 1, 2)
        own = own.reshape(AB, own.shape[1], 3 * channels)
        own = jnp.pad(own, ((0, 0), (0, 0), (0, 2 * HALF - 3 * channels)))
        oth = shift(own, "core", 1)
        rows = jnp.where(core == 0, jnp.concatenate([own, oth], axis=1), jnp.concatenate([oth, own], axis=1))
        half = jnp.where(core == 0, rows[:, :, :HALF], rows[:, :, HALF:])
        spread = jnp.broadcast_to(half[None], (chips, *half.shape))
        b_own = lax.all_to_all(spread, CHIPS, 0, 0, tiled=True)
        b_own = b_own.reshape(-1, HALF)
        b_oth = shift(b_own, "core", 1)

    with jax.named_scope("gather_basis_g"):
        bg = lax.all_gather(basis_g.T, ALL, axis=0)
        bg = bg.reshape(-1, tensor, *bg.shape[1:])

    with jax.named_scope("exchange_grads"):
        grads_all = lax.all_to_all(grads, "z", 0, 0, tiled=True)

    def part(s, dtype):
        idx = jnp.stack([core, (z + s) % tensor]).astype(jnp.int32)
        return conv(idx, b_own, b_oth, x, per, dtype)

    received = []
    for s in (2, 1, 3):
        with jax.named_scope("coeff_part"):
            received.append(shift(part(s, jnp.bfloat16), "z", s))
    mine = part(0, jnp.float32)

    examples = here * lax.axis_size(("x", "y", "core"))
    total = squares(mine, received, grads_all, bg, 1.0 / examples)

    with jax.named_scope("sum_examples"):
        rows = total.reshape(chips, 2, -1, total.shape[1])
        keep = jnp.where(core == 0, rows[:, 0], rows[:, 1])
        give = jnp.where(core == 0, rows[:, 1], rows[:, 0])
        keep = keep + shift(give, "core", 1)
        keep = keep.astype(jnp.bfloat16).reshape(chips * tensor, 1, -1)
        got = lax.all_to_all(keep, ("x", "y", "z"), 0, 0, tiled=True)
        return jnp.sum(got.astype(jnp.float32), axis=0)


def solution(mesh):
    tensor = mesh.shape["tensor"]
    fine = Mesh(mesh.devices.reshape(4, -1, 2, tensor), ALL)
    dp = ("x", "y", "core")
    in_specs = (P(dp, None, "z"), P(dp, None, "z"), P(None, "z", dp), P("z", dp))
    return jax.shard_map(body, mesh=fine, in_specs=in_specs, out_specs=P(ALL, None), check_vma=False)
```

```python
import jax
import jax.numpy as jnp
from jax import lax
from jax.experimental import pallas as pl
from jax.experimental.pallas import tpu as pltpu
from jax.sharding import Mesh, PartitionSpec as P

SIDE = 8
POS = SIDE * SIDE * SIDE
AB = 9
ALL = ("x", "y", "core", "z")
NT = (((1,), (1,)), ((), ()))
VMEM = pl.BlockSpec(memory_space=pltpu.VMEM)
SMEM = pl.BlockSpec(memory_space=pltpu.SMEM)
HBM = pl.BlockSpec(memory_space=pltpu.HBM)


def lane_coords():
    p = lax.broadcasted_iota(jnp.int32, (1, POS), 1)
    return p // 64, (p // 8) % 8, p % 8


def shifted(y, ab, i, j):
    a, b = ab // 3 - 1, ab % 3 - 1
    s = a * 64 + b * 8
    if s == 0:
        return y
    ok = None
    for v, o in ((i, a), (j, b)):
        if o != 0:
            m = (v + o >= 0) & (v + o < SIDE)
            ok = m if ok is None else ok & m
    return jnp.where(ok, pltpu.roll(y, (-s) % POS, 1), 0.0)


def conv_kernel(idx_ref, *refs):
    *b_refs, x_ref, x_oth_ref, o_ref, b_buf, x_buf, xc_ref, o_buf, sem = refs
    i, j, k = lane_coords()
    block = idx_ref[0]
    h = x_ref.shape[1]
    per = o_ref.shape[0] // 2
    parts, rows = len(b_refs), b_refs[0].shape[1]
    copies = [
        pltpu.make_async_copy(ref.at[block * per + n], x_buf.at[m * per + n], sem.at[m * per + n])
        for m, ref in enumerate((x_ref, x_oth_ref))
        for n in range(per)
    ]
    loads = [pltpu.make_async_copy(ref, b_buf.at[m], sem.at[2 * per + m]) for m, ref in enumerate(b_refs)]
    for c in copies[:1] + loads + copies[1:]:
        c.start()
    b, stores = None, []
    for n in range(2 * per):
        copies[n].wait()
        x = x_buf[n]
        xf = x.astype(jnp.float32)
        xc_ref[:h] = jnp.where(k >= 1, pltpu.roll(xf, 1, 1), 0.0).astype(x.dtype)
        xc_ref[h : 2 * h] = x
        xc_ref[2 * h :] = jnp.where(k <= SIDE - 2, pltpu.roll(xf, POS - 1, 1), 0.0).astype(x.dtype)
        if b is None:
            for c in loads:
                c.wait()
            b = b_buf[...].reshape(parts * AB * rows, 3 * h)
        y = jnp.dot(b, xc_ref[...], preferred_element_type=jnp.float32)
        y = y.reshape(parts, AB, rows, POS)
        acc = None
        for ab in range(AB):
            t = shifted(y[:, ab].reshape(-1, POS), ab, i, j)
            acc = t if acc is None else acc + t
        o_buf[n] = acc.astype(o_ref.dtype)
        stores.append(pltpu.make_async_copy(o_buf.at[n], o_ref.at[n], sem.at[2 * per + parts + n]))
        stores[-1].start()
    for c in stores:
        c.wait()


def conv(idx, blocks, x, x_oth, per, dtype):
    rows = blocks[0].shape[1]
    ranks = len(blocks) * rows
    return pl.pallas_call(
        conv_kernel,
        out_shape=jax.ShapeDtypeStruct((2 * per, ranks, POS), dtype),
        in_specs=[SMEM] + [HBM] * (len(blocks) + 2),
        out_specs=HBM,
        scratch_shapes=[
            pltpu.VMEM((len(blocks), *blocks[0].shape), jnp.bfloat16),
            pltpu.VMEM((2 * per, x.shape[1], POS), jnp.bfloat16),
            pltpu.VMEM((3 * x.shape[1], POS), jnp.bfloat16),
            pltpu.VMEM((2 * per, ranks, POS), dtype),
            pltpu.SemaphoreType.DMA((4 * per + len(blocks),)),
        ],
        compiler_params=pltpu.CompilerParams(vmem_limit_bytes=40 << 20),
        name="conv_taps",
    )(idx, *blocks, x, x_oth)


def squares_kernel(idx_ref, own_ref, r1_ref, r2_ref, r3_ref, g_ref, g_oth_ref, bg_ref, bg_oth_ref, o_ref, own_buf, r_buf, g_buf, bg_buf, hi_ref, m_ref, sem, *, scale):
    x, y, core, z = idx_ref[0], idx_ref[1], idx_ref[2], idx_ref[3]
    chips, width = bg_ref.shape[0], bg_ref.shape[1]
    examples, ranks = own_ref.shape[0], own_ref.shape[1]
    per = examples // 2
    tensor = g_ref.shape[0] // per
    side = 4

    def chip(rx, ry):
        return ((x + side - rx) % side) * side + (y + side - ry) % side

    pairs = [(own_ref, own_buf), (r1_ref, r_buf.at[0]), (r2_ref, r_buf.at[1]), (r3_ref, r_buf.at[2])]
    for n in range(examples):
        src = g_ref if n < per else g_oth_ref
        for t in range(tensor):
            pairs.append((src.at[((z + tensor - t) % tensor) * per + n % per], g_buf.at[n, t]))
    late = len(pairs)
    for b in range(chips):
        at = chip(b // side, b % side) * 2
        pairs.append((bg_ref.at[b], bg_buf.at[at + core]))
        pairs.append((bg_oth_ref.at[b], bg_buf.at[at + 1 - core]))
    copies = [pltpu.make_async_copy(a, b, sem.at[i]) for i, (a, b) in enumerate(pairs)]
    for c in copies:
        c.start()
    for c in copies[:4]:
        c.wait()
    for n in range(examples):
        c = own_buf[n] + r_buf[0, n].astype(jnp.float32) + r_buf[1, n].astype(jnp.float32) + r_buf[2, n].astype(jnp.float32)
        hi_ref[n] = c.astype(jnp.bfloat16)
        hi = hi_ref[n]
        lo = (c - hi.astype(jnp.float32)).astype(jnp.bfloat16)
        both = jnp.concatenate([hi, lo], axis=0)
        for c in copies[4 + n * tensor : 4 + (n + 1) * tensor]:
            c.wait()
        g = g_buf[n].reshape(-1, POS)
        m = lax.dot_general(both, g, NT, preferred_element_type=jnp.float32)
        m_ref[n * ranks : (n + 1) * ranks] = (m[:ranks] + m[ranks:]).astype(jnp.bfloat16)
    for c in copies[late:]:
        c.wait()
    bg = bg_buf[...].reshape(2 * chips * width, bg_buf.shape[2])
    prod = lax.dot_general(m_ref[...], bg, NT, preferred_element_type=jnp.float32)
    sq = None
    for n in range(examples):
        t = prod[n * ranks : (n + 1) * ranks]
        sq = t * t if sq is None else sq + t * t
    sq = sq * scale
    low = ranks // chips
    for b in range(chips):
        o_ref[chip(b % side, b // side)] = sq[b * low : (b + 1) * low]


def squares(idx, own, received, g, g_oth, bg, bg_oth, scale):
    examples, ranks = own.shape[0], own.shape[1]
    chips, width, hidden = bg.shape
    tensor = g.shape[0] // (examples // 2)

    def kernel(*refs):
        squares_kernel(*refs, scale=scale)

    return pl.pallas_call(
        kernel,
        out_shape=jax.ShapeDtypeStruct((chips, ranks // chips, 2 * chips * width), jnp.float32),
        in_specs=[SMEM] + [HBM] * 8,
        out_specs=VMEM,
        scratch_shapes=[
            pltpu.VMEM(own.shape, jnp.float32),
            pltpu.VMEM((3, *own.shape), jnp.bfloat16),
            pltpu.VMEM((examples, tensor, *g.shape[1:]), jnp.bfloat16),
            pltpu.VMEM((2 * chips, width, hidden), jnp.bfloat16),
            pltpu.VMEM((examples, ranks, POS), jnp.bfloat16),
            pltpu.VMEM((examples * ranks, hidden), jnp.bfloat16),
            pltpu.SemaphoreType.DMA((4 + examples * tensor + 2 * chips,)),
        ],
        compiler_params=pltpu.CompilerParams(vmem_limit_bytes=48 << 20),
        name="squared_sums",
    )(idx, own, *received, g, g_oth, bg, bg_oth)


def shift(v, axis, s):
    n = lax.axis_size(axis)
    return lax.ppermute(v, axis, [(i, (i + s) % n) for i in range(n)])


def around(v, axis):
    return [v] + [shift(v, axis, s) for s in range(1, lax.axis_size(axis))]


def body(patch_rows, out_grads, basis_a, basis_g):
    coords = [lax.axis_index(a).astype(jnp.int32) for a in ALL]
    z = coords[3]
    x = patch_rows.transpose(0, 2, 1)
    grads = out_grads.transpose(0, 2, 1)
    here, channels = x.shape[0], x.shape[1]
    tensor = lax.axis_size("z")
    per = here // tensor

    with jax.named_scope("basis_g_z"):
        bg = around(basis_g.T, "z")
    with jax.named_scope("basis_a_x"):
        own = basis_a.reshape(AB, 3, channels, -1).transpose(0, 3, 1, 2)
        ba = around(own.reshape(AB, own.shape[1], 3 * channels), "x")
    with jax.named_scope("exchange_grads"):
        g = lax.all_to_all(grads, "z", 0, 0, tiled=True)
    with jax.named_scope("exchange_inputs"):
        x_oth = shift(x, "core", 1)

    ba, bg, x_oth = lax.optimization_barrier((ba, bg, x_oth))
    with jax.named_scope("basis_a_y"):
        ba = around(jnp.concatenate(ba, axis=1), "y")
    with jax.named_scope("basis_g_y"):
        bg = around(jnp.concatenate(bg, axis=1), "y")

    ba, bg = lax.optimization_barrier((ba, bg))
    with jax.named_scope("basis_g_x"):
        bg = around(jnp.stack(bg), "x")

    parts = []

    def part(s, dtype):
        idx = ((z + s) % tensor).reshape(1)
        if parts:
            idx, _ = lax.optimization_barrier((idx, parts[-1]))
        return conv(idx, ba, x, x_oth, per, dtype)

    received = []
    for s in (2, 1, 3):
        with jax.named_scope("coeff_part"):
            parts.append(part(s, jnp.bfloat16))
            received.append(shift(parts[-1], "z", s))
    parts.append(received[0])
    mine = part(0, jnp.float32)
    with jax.named_scope("exchange_cores"):
        g, bg, _ = lax.optimization_barrier((g, bg, parts[2]))
        g_oth = shift(g, "core", 1)
        bg = jnp.concatenate(bg, axis=0)
        bg_oth = shift(bg, "core", 1)

    examples = here * lax.axis_size(("x", "y", "core"))
    total = squares(jnp.stack(coords), mine, received, g, g_oth, bg, bg_oth, 1.0 / examples)

    with jax.named_scope("sum_examples"):
        rows = total.reshape(-1, 1, total.shape[2])
        got = lax.all_to_all(rows, ("x", "y", "z"), 0, 0, tiled=True)
        return jnp.sum(got, axis=0)


def solution(mesh):
    tensor = mesh.shape["tensor"]
    fine = Mesh(mesh.devices.reshape(4, -1, 2, tensor), ALL)
    dp = ("x", "y", "core")
    in_specs = (P(dp, None, "z"), P(dp, None, "z"), P(None, "z", dp), P("z", dp))
    return jax.shard_map(body, mesh=fine, in_specs=in_specs, out_specs=P(ALL, None), check_vma=False)
```

```python
import jax
import jax.numpy as jnp
from jax import lax
from jax.experimental import pallas as pl
from jax.experimental.pallas import tpu as pltpu
from jax.sharding import Mesh, PartitionSpec as P

SIDE = 8
POS = SIDE * SIDE * SIDE
AB = 9
ALL = ("x", "y", "core", "z")
NT = (((1,), (1,)), ((), ()))
VMEM = pl.BlockSpec(memory_space=pltpu.VMEM)
SMEM = pl.BlockSpec(memory_space=pltpu.SMEM)
HBM = pl.BlockSpec(memory_space=pltpu.HBM)


def lane_coords():
    p = lax.broadcasted_iota(jnp.int32, (1, POS), 1)
    return p // 64, (p // 8) % 8, p % 8


def shifted(y, ab, i, j):
    a, b = ab // 3 - 1, ab % 3 - 1
    s = a * 64 + b * 8
    if s == 0:
        return y
    ok = None
    for v, o in ((i, a), (j, b)):
        if o != 0:
            m = (v + o >= 0) & (v + o < SIDE)
            ok = m if ok is None else ok & m
    return jnp.where(ok, pltpu.roll(y, (-s) % POS, 1), 0.0)


def conv_kernel(idx_ref, *refs):
    *b_refs, x_ref, x_oth_ref, o_ref, xc_ref, o_buf, sem = refs
    i, j, k = lane_coords()
    block = idx_ref[0]
    h = x_ref.shape[1]
    per = o_ref.shape[0] // 2
    rows = b_refs[0].shape[1]
    zero = jnp.zeros((), x_ref.dtype)
    b = jnp.concatenate([r[...].reshape(AB * rows, 3 * h) for r in b_refs], axis=0)
    for n in range(2 * per):
        x = (x_ref if n < per else x_oth_ref)[block * per + n % per]
        xc_ref[n, :h] = jnp.where(k >= 1, pltpu.roll(x, 1, 1), zero)
        xc_ref[n, h : 2 * h] = x
        xc_ref[n, 2 * h :] = jnp.where(k <= SIDE - 2, pltpu.roll(x, POS - 1, 1), zero)
    stores = []
    for n in range(2 * per):
        y = jnp.dot(b, xc_ref[n], preferred_element_type=jnp.float32)
        y = y.reshape(len(b_refs), AB, rows, POS)
        acc = None
        for ab in range(AB):
            t = shifted(y[:, ab].reshape(-1, POS), ab, i, j)
            acc = t if acc is None else acc + t
        o_buf[n] = acc.astype(o_ref.dtype)
        stores.append(pltpu.make_async_copy(o_buf.at[n], o_ref.at[n], sem.at[n]))
        stores[-1].start()
    for c in stores:
        c.wait()


def conv(idx, blocks, x, x_oth, per, dtype):
    ranks = len(blocks) * blocks[0].shape[1]
    return pl.pallas_call(
        conv_kernel,
        out_shape=jax.ShapeDtypeStruct((2 * per, ranks, POS), dtype),
        in_specs=[SMEM] + [VMEM] * (len(blocks) + 2),
        out_specs=HBM,
        scratch_shapes=[
            pltpu.VMEM((2 * per, 3 * x.shape[1], POS), jnp.bfloat16),
            pltpu.VMEM((2 * per, ranks, POS), dtype),
            pltpu.SemaphoreType.DMA((2 * per,)),
        ],
        compiler_params=pltpu.CompilerParams(vmem_limit_bytes=18 << 20),
        name="conv_taps",
    )(idx, *blocks, x, x_oth)


def merge_kernel(*refs):
    *parts, o_ref, sem = refs
    copies = [pltpu.make_async_copy(p, o_ref.at[i], sem.at[i]) for i, p in enumerate(parts)]
    for c in copies:
        c.start()
    for c in copies:
        c.wait()


def merge(parts):
    return pl.pallas_call(
        merge_kernel,
        out_shape=jax.ShapeDtypeStruct((len(parts), *parts[0].shape), parts[0].dtype),
        in_specs=[HBM] * len(parts),
        out_specs=HBM,
        scratch_shapes=[pltpu.SemaphoreType.DMA((len(parts),))],
        name="stack_copies",
    )(*parts)


def squares_kernel(idx_ref, own_ref, r1_ref, r2_ref, r3_ref, g_ref, g_oth_ref, bg_ref, bg_oth_ref, o_ref, own_buf, r_buf, g_buf, bg_buf, hi_ref, m_ref, sem, *, scale):
    x, y, core, z = idx_ref[0], idx_ref[1], idx_ref[2], idx_ref[3]
    side, width = bg_ref.shape[0], bg_ref.shape[2]
    examples, ranks = own_ref.shape[0], own_ref.shape[1]
    per = examples // 2
    tensor = g_ref.shape[0] // per

    def chip(rx, ry):
        return ((x + side - rx) % side) * side + (y + side - ry) % side

    pairs = [(own_ref, own_buf)] + [(r, r_buf.at[i]) for i, r in enumerate((r1_ref, r2_ref, r3_ref))]
    for n in range(examples):
        src = g_ref if n < per else g_oth_ref
        for t in range(tensor):
            pairs.append((src.at[((z + tensor - t) % tensor) * per + n % per], g_buf.at[n, t]))
    late = len(pairs)
    for rx in range(side):
        for ry in range(side):
            at = chip(rx, ry) * 2
            pairs.append((bg_ref.at[rx, ry], bg_buf.at[at + core]))
            pairs.append((bg_oth_ref.at[rx, ry], bg_buf.at[at + 1 - core]))
    copies = [pltpu.make_async_copy(p, q, sem.at[i]) for i, (p, q) in enumerate(pairs)]
    for c in copies:
        c.start()
    for c in copies[:4]:
        c.wait()
    for n in range(examples):
        c = own_buf[n] + r_buf[0, n].astype(jnp.float32) + r_buf[1, n].astype(jnp.float32) + r_buf[2, n].astype(jnp.float32)
        hi_ref[n] = c.astype(jnp.bfloat16)
        hi = hi_ref[n]
        lo = (c - hi.astype(jnp.float32)).astype(jnp.bfloat16)
        both = jnp.concatenate([hi, lo], axis=0)
        for c in copies[4 + n * tensor : 4 + (n + 1) * tensor]:
            c.wait()
        m = lax.dot_general(both, g_buf[n].reshape(-1, POS), NT, preferred_element_type=jnp.float32)
        m_ref[n * ranks : (n + 1) * ranks] = (m[:ranks] + m[ranks:]).astype(jnp.bfloat16)
    for c in copies[late:]:
        c.wait()
    bg = bg_buf[...].reshape(bg_buf.shape[0] * width, bg_buf.shape[2])
    prod = lax.dot_general(m_ref[...], bg, NT, preferred_element_type=jnp.float32)
    sq = None
    for n in range(examples):
        t = prod[n * ranks : (n + 1) * ranks]
        sq = t * t if sq is None else sq + t * t
    sq = sq * scale
    low = ranks // (side * side)
    for b in range(side * side):
        o_ref[chip(b % side, b // side)] = sq[b * low : (b + 1) * low]


def squares(idx, own, received, g, g_oth, bg, bg_oth, scale):
    examples, ranks = own.shape[0], own.shape[1]
    side, _, width, hidden = bg.shape
    chips = side * side
    tensor = g.shape[0] // (examples // 2)

    def kernel(*refs):
        squares_kernel(*refs, scale=scale)

    return pl.pallas_call(
        kernel,
        out_shape=jax.ShapeDtypeStruct((chips, ranks // chips, 2 * chips * width), jnp.float32),
        in_specs=[SMEM] + [HBM] * 8,
        out_specs=VMEM,
        scratch_shapes=[
            pltpu.VMEM(own.shape, jnp.float32),
            pltpu.VMEM((3, *own.shape), jnp.bfloat16),
            pltpu.VMEM((examples, tensor, *g.shape[1:]), jnp.bfloat16),
            pltpu.VMEM((2 * chips, width, hidden), jnp.bfloat16),
            pltpu.VMEM((examples, ranks, POS), jnp.bfloat16),
            pltpu.VMEM((examples * ranks, hidden), jnp.bfloat16),
            pltpu.SemaphoreType.DMA((4 + examples * tensor + 2 * chips,)),
        ],
        compiler_params=pltpu.CompilerParams(vmem_limit_bytes=28 << 20),
        name="squared_sums",
    )(idx, own, *received, g, g_oth, bg, bg_oth)


def shift(v, axis, s):
    n = lax.axis_size(axis)
    return lax.ppermute(v, axis, [(i, (i + s) % n) for i in range(n)])


def around(v, axis):
    return [v] + [shift(v, axis, s) for s in range(1, lax.axis_size(axis))]


def body(patch_rows, out_grads, basis_a, basis_g):
    coords = [lax.axis_index(a).astype(jnp.int32) for a in ALL]
    z = coords[3]
    x = patch_rows.transpose(0, 2, 1)
    grads = out_grads.transpose(0, 2, 1)
    here, channels = x.shape[0], x.shape[1]
    tensor = lax.axis_size("z")
    per = here // tensor

    with jax.named_scope("basis_g_z"):
        bg = around(basis_g.T, "z")
    with jax.named_scope("basis_a_x"):
        own = basis_a.reshape(AB, 3, channels, -1).transpose(0, 3, 1, 2)
        own = own.reshape(AB, own.shape[1], 3 * channels)
        grads, bg, own = lax.optimization_barrier((grads, bg, own))
        ba = around(own, "x")
    with jax.named_scope("exchange_grads"):
        g = lax.all_to_all(grads, "z", 0, 0, tiled=True)
    with jax.named_scope("exchange_inputs"):
        x_oth = shift(x, "core", 1)

    with jax.named_scope("basis_a_y"):
        ba = jnp.concatenate(ba, axis=1)
        ba, bg, x_oth = lax.optimization_barrier((ba, bg, x_oth))
        ba = around(ba, "y")
    with jax.named_scope("basis_g_y"):
        bg = around(jnp.concatenate(bg, axis=1), "y")

    ba, bg = lax.optimization_barrier((ba, bg))
    with jax.named_scope("basis_g_x"):
        bg = around(jnp.stack(bg), "x")

    parts = []

    def part(s, dtype):
        idx = ((z + s) % tensor).reshape(1)
        if parts:
            idx, _ = lax.optimization_barrier((idx, parts[-1]))
        return conv(idx, ba, x, x_oth, per, dtype)

    received = []
    for s in (2, 1, 3):
        with jax.named_scope("coeff_part"):
            parts.append(part(s, jnp.bfloat16))
            received.append(shift(parts[-1], "z", s))
    parts.append((parts[-1], received[0]))
    mine = part(0, jnp.float32)
    with jax.named_scope("exchange_cores"):
        g, bg, mine = lax.optimization_barrier((g, bg, mine))
        g_oth = shift(g, "core", 1)
        bg = merge(bg)
        bg_oth = shift(bg, "core", 1)

    examples = here * lax.axis_size(("x", "y", "core"))
    total = squares(jnp.stack(coords), mine, received, g, g_oth, bg, bg_oth, 1.0 / examples)

    with jax.named_scope("sum_examples"):
        rows = total.reshape(-1, 1, total.shape[2])
        got = lax.all_to_all(rows, ("x", "y", "z"), 0, 0, tiled=True)
        return jnp.sum(got, axis=0)


def solution(mesh):
    tensor = mesh.shape["tensor"]
    fine = Mesh(mesh.devices.reshape(4, -1, 2, tensor), ALL)
    dp = ("x", "y", "core")
    in_specs = (P(dp, None, "z"), P(dp, None, "z"), P(None, "z", dp), P("z", dp))
    return jax.shard_map(body, mesh=fine, in_specs=in_specs, out_specs=P(ALL, None), check_vma=False)
```

```python
import jax
import jax.numpy as jnp
from jax import lax
from jax.experimental import pallas as pl
from jax.experimental.pallas import tpu as pltpu
from jax.sharding import Mesh, PartitionSpec as P

SIDE = 8
POS = SIDE * SIDE * SIDE
AB = 9
ALL = ("x", "y", "core", "z")
NT = (((1,), (1,)), ((), ()))
VMEM = pl.BlockSpec(memory_space=pltpu.VMEM)
SMEM = pl.BlockSpec(memory_space=pltpu.SMEM)
ANY = pl.BlockSpec(memory_space=pl.ANY)


def lane_coords():
    p = lax.broadcasted_iota(jnp.int32, (1, POS), 1)
    return p // 64, (p // 8) % 8, p % 8


def shifted(y, ab, i, j):
    a, b = ab // 3 - 1, ab % 3 - 1
    s = a * 64 + b * 8
    if s == 0:
        return y
    ok = None
    for v, o in ((i, a), (j, b)):
        if o != 0:
            m = (v + o >= 0) & (v + o < SIDE)
            ok = m if ok is None else ok & m
    return jnp.where(ok, pltpu.roll(y, (-s) % POS, 1), 0.0)


def conv_kernel(idx_ref, *refs, outs):
    b_refs, (x_ref, x_oth_ref), o_refs = refs[:-6 - outs], refs[-6 - outs : -4 - outs], refs[-4 - outs : -4]
    b_buf, x_buf, xc_ref, sem = refs[-4:]
    i, j, k = lane_coords()
    h = x_ref.shape[1]
    per = o_refs[0].shape[0] // 2
    parts, rows = len(b_refs), b_refs[0].shape[1]
    zero = jnp.zeros((), x_ref.dtype)
    pairs = [(r, b_buf.at[m]) for m, r in enumerate(b_refs)]
    for o in range(outs):
        for m, ref in enumerate((x_ref, x_oth_ref)):
            for n in range(per):
                pairs.append((ref.at[idx_ref[o] * per + n], x_buf.at[(2 * o + m) * per + n]))
    copies = [pltpu.make_async_copy(p, q, sem.at[t]) for t, (p, q) in enumerate(pairs)]
    for c in copies:
        c.start()
    b = None
    for n in range(2 * per * outs):
        copies[parts + n].wait()
        x = x_buf[n]
        xc_ref[n % 2, :h] = jnp.where(k >= 1, pltpu.roll(x, 1, 1), zero)
        xc_ref[n % 2, h : 2 * h] = x
        xc_ref[n % 2, 2 * h :] = jnp.where(k <= SIDE - 2, pltpu.roll(x, POS - 1, 1), zero)
        if b is None:
            for c in copies[:parts]:
                c.wait()
            b = b_buf[...].reshape(parts * AB * rows, 3 * h)
        y = jnp.dot(b, xc_ref[n % 2], preferred_element_type=jnp.float32)
        y = y.reshape(parts, AB, rows, POS)
        acc = None
        for ab in range(AB):
            t = shifted(y[:, ab].reshape(-1, POS), ab, i, j)
            acc = t if acc is None else acc + t
        o_ref = o_refs[n // (2 * per)]
        o_ref[n % (2 * per)] = acc.astype(o_ref.dtype)


def conv(idx, blocks, x, x_oth, per, dtypes):
    ranks = len(blocks) * blocks[0].shape[1]
    outs = len(dtypes)
    examples = 2 * per * outs

    def kernel(*refs):
        conv_kernel(*refs, outs=outs)

    return pl.pallas_call(
        kernel,
        out_shape=[jax.ShapeDtypeStruct((2 * per, ranks, POS), d) for d in dtypes],
        in_specs=[SMEM] + [ANY] * (len(blocks) + 2),
        out_specs=[VMEM] * outs,
        scratch_shapes=[
            pltpu.VMEM((len(blocks), *blocks[0].shape), jnp.bfloat16),
            pltpu.VMEM((examples, *x.shape[1:]), jnp.bfloat16),
            pltpu.VMEM((2, 3 * x.shape[1], POS), jnp.bfloat16),
            pltpu.SemaphoreType.DMA((len(blocks) + examples,)),
        ],
        compiler_params=pltpu.CompilerParams(vmem_limit_bytes=48 << 20),
        name="conv_taps",
    )(idx, *blocks, x, x_oth)


def squares_kernel(idx_ref, own_ref, r1_ref, r2_ref, r3_ref, g_ref, g_oth_ref, *refs, scale):
    *bg_refs, o_ref, own_buf, r_buf, g_buf, bg_buf, hi_ref, m_ref, sem = refs
    x, y, core, z = idx_ref[0], idx_ref[1], idx_ref[2], idx_ref[3]
    side, width = len(bg_refs) // 2, bg_refs[0].shape[1]
    examples, ranks = own_ref.shape[0], own_ref.shape[1]
    per = examples // 2
    tensor = g_ref.shape[0] // per

    def chip(rx, ry):
        return ((x + side - rx) % side) * side + (y + side - ry) % side

    pairs = [(own_ref, own_buf)] + [(r, r_buf.at[i]) for i, r in enumerate((r1_ref, r2_ref, r3_ref))]
    for n in range(examples):
        src = g_ref if n < per else g_oth_ref
        for t in range(tensor):
            pairs.append((src.at[((z + tensor - t) % tensor) * per + n % per], g_buf.at[n, t]))
    late = len(pairs)
    for rx in range(side):
        for ry in range(side):
            at = chip(rx, ry) * 2
            pairs.append((bg_refs[ry].at[rx], bg_buf.at[at + core]))
            pairs.append((bg_refs[side + ry].at[rx], bg_buf.at[at + 1 - core]))
    copies = [pltpu.make_async_copy(p, q, sem.at[i]) for i, (p, q) in enumerate(pairs)]
    for c in copies:
        c.start()
    for c in copies[:4]:
        c.wait()
    for n in range(examples):
        c = own_buf[n] + r_buf[0, n].astype(jnp.float32) + r_buf[1, n].astype(jnp.float32) + r_buf[2, n].astype(jnp.float32)
        hi_ref[n] = c.astype(jnp.bfloat16)
        hi = hi_ref[n]
        lo = (c - hi.astype(jnp.float32)).astype(jnp.bfloat16)
        both = jnp.concatenate([hi, lo], axis=0)
        for c in copies[4 + n * tensor : 4 + (n + 1) * tensor]:
            c.wait()
        m = lax.dot_general(both, g_buf[n].reshape(-1, POS), NT, preferred_element_type=jnp.float32)
        m_ref[n * ranks : (n + 1) * ranks] = (m[:ranks] + m[ranks:]).astype(jnp.bfloat16)
    for c in copies[late:]:
        c.wait()
    bg = bg_buf[...].reshape(bg_buf.shape[0] * width, bg_buf.shape[2])
    prod = lax.dot_general(m_ref[...], bg, NT, preferred_element_type=jnp.float32)
    sq = None
    for n in range(examples):
        t = prod[n * ranks : (n + 1) * ranks]
        sq = t * t if sq is None else sq + t * t
    sq = sq * scale
    low = ranks // (side * side)
    for b in range(side * side):
        o_ref[chip(b % side, b // side)] = sq[b * low : (b + 1) * low]


def squares(idx, own, received, g, g_oth, bg, bg_oth, scale):
    examples, ranks = own.shape[0], own.shape[1]
    side, width, hidden = bg[0].shape
    chips = side * side
    tensor = g.shape[0] // (examples // 2)

    def kernel(*refs):
        squares_kernel(*refs, scale=scale)

    return pl.pallas_call(
        kernel,
        out_shape=jax.ShapeDtypeStruct((chips, ranks // chips, 2 * chips * width), jnp.float32),
        in_specs=[SMEM] + [ANY] * (6 + 2 * side),
        out_specs=VMEM,
        scratch_shapes=[
            pltpu.VMEM(own.shape, jnp.float32),
            pltpu.VMEM((3, *own.shape), jnp.bfloat16),
            pltpu.VMEM((examples, tensor, *g.shape[1:]), jnp.bfloat16),
            pltpu.VMEM((2 * chips, width, hidden), jnp.bfloat16),
            pltpu.VMEM((examples, ranks, POS), jnp.bfloat16),
            pltpu.VMEM((examples * ranks, hidden), jnp.bfloat16),
            pltpu.SemaphoreType.DMA((4 + examples * tensor + 2 * chips,)),
        ],
        compiler_params=pltpu.CompilerParams(vmem_limit_bytes=48 << 20),
        name="squared_sums",
    )(idx, own, *received, g, g_oth, *bg, *bg_oth)


def shift(v, axis, s):
    n = lax.axis_size(axis)
    return lax.ppermute(v, axis, [(i, (i + s) % n) for i in range(n)])


def around(v, axis):
    return [v] + [shift(v, axis, s) for s in range(1, lax.axis_size(axis))]


def body(patch_rows, out_grads, basis_a, basis_g):
    coords = [lax.axis_index(a).astype(jnp.int32) for a in ALL]
    z = coords[3]
    x = patch_rows.transpose(0, 2, 1)
    grads = out_grads.transpose(0, 2, 1)
    here, channels = x.shape[0], x.shape[1]
    tensor = lax.axis_size("z")
    per = here // tensor

    with jax.named_scope("basis_a_x"):
        own = basis_a.reshape(AB, 3, channels, -1).transpose(0, 3, 1, 2)
        own = own.reshape(AB, own.shape[1], 3 * channels)
        ba = around(own, "x")
    with jax.named_scope("basis_g_z"):
        bg, _ = lax.optimization_barrier((basis_g.T, own))
        bg = around(bg, "z")
    with jax.named_scope("exchange_grads"):
        grads, bg, ba = lax.optimization_barrier((grads, bg, ba))
        g = lax.all_to_all(grads, "z", 0, 0, tiled=True)
    with jax.named_scope("basis_a_y"):
        ba = jnp.concatenate(ba, axis=1)
        bg, give, _ = lax.optimization_barrier((bg, x, ba))
        x_oth = shift(give, "core", 1)
        ba = around(ba, "y")
    with jax.named_scope("basis_g_x"):
        bg = around(jnp.concatenate(bg, axis=1), "x")

    def parts(shifts, dtypes, after=None):
        idx = jnp.stack([(z + s) % tensor for s in shifts])
        if after is not None:
            idx, _ = lax.optimization_barrier((idx, after))
        return conv(idx, ba, x, x_oth, per, dtypes)

    ba, bg = lax.optimization_barrier((ba, bg))
    with jax.named_scope("basis_g_y"):
        bg = around(jnp.stack(bg), "y")
    with jax.named_scope("coeff_parts"):
        far, near = parts((2, 1), (jnp.bfloat16, jnp.bfloat16))
        received = [shift(far, "z", 2), shift(near, "z", 1)]
        last, mine = parts((3, 0), (jnp.bfloat16, jnp.float32), far)
    with jax.named_scope("exchange_cores"):
        g, bg, received, mine = lax.optimization_barrier((g, bg, received, mine))
        g_oth = shift(g, "core", 1)
        bg_oth = [shift(v, "core", 1) for v in bg]
    received.append(shift(last, "z", 3))

    examples = here * lax.axis_size(("x", "y", "core"))
    total = squares(jnp.stack(coords), mine, received, g, g_oth, bg, bg_oth, 1.0 / examples)

    with jax.named_scope("sum_examples"):
        rows = total.reshape(-1, 1, total.shape[2])
        got = lax.all_to_all(rows, ("x", "y", "z"), 0, 0, tiled=True)
        return jnp.sum(got, axis=0)


def solution(mesh):
    tensor = mesh.shape["tensor"]
    fine = Mesh(mesh.devices.reshape(4, -1, 2, tensor), ALL)
    dp = ("x", "y", "core")
    in_specs = (P(dp, None, "z"), P(dp, None, "z"), P(None, "z", dp), P("z", dp))
    return jax.shard_map(body, mesh=fine, in_specs=in_specs, out_specs=P(ALL, None), check_vma=False)
```

```python
import jax
import jax.numpy as jnp
from jax import lax
from jax.experimental import pallas as pl
from jax.experimental.pallas import tpu as pltpu
from jax.sharding import Mesh, PartitionSpec as P

SIDE = 8
POS = SIDE * SIDE * SIDE
AB = 9
ALL = ("x", "y", "core", "z")
NT = (((1,), (1,)), ((), ()))
VMEM = pl.BlockSpec(memory_space=pltpu.VMEM)
SMEM = pl.BlockSpec(memory_space=pltpu.SMEM)


def lane_coords():
    p = lax.broadcasted_iota(jnp.int32, (1, POS), 1)
    return p // 64, (p // 8) % 8, p % 8


def shifted(y, ab, i, j):
    a, b = ab // 3 - 1, ab % 3 - 1
    s = a * 64 + b * 8
    if s == 0:
        return y
    ok = None
    for v, o in ((i, a), (j, b)):
        if o != 0:
            m = (v + o >= 0) & (v + o < SIDE)
            ok = m if ok is None else ok & m
    return jnp.where(ok, pltpu.roll(y, (-s) % POS, 1), 0.0)


def conv_kernel(idx_ref, b_ref, x_ref, x_oth_ref, *refs):
    *o_refs, xc_ref = refs
    i, j, k = lane_coords()
    h = x_ref.shape[1]
    per = o_refs[0].shape[0] // 2
    ranks = b_ref.shape[1]
    zero = jnp.zeros((), x_ref.dtype)
    b = b_ref[...].reshape(AB * ranks, 3 * h)
    for n in range(2 * per * len(o_refs)):
        o, m = n // (2 * per), n % (2 * per)
        x = (x_ref if m < per else x_oth_ref)[idx_ref[o] * per + m % per]
        xc_ref[n % 2, :h] = jnp.where(k >= 1, pltpu.roll(x, 1, 1), zero)
        xc_ref[n % 2, h : 2 * h] = x
        xc_ref[n % 2, 2 * h :] = jnp.where(k <= SIDE - 2, pltpu.roll(x, POS - 1, 1), zero)
        y = jnp.dot(b, xc_ref[n % 2], preferred_element_type=jnp.float32)
        acc = None
        for ab in range(AB):
            t = shifted(y[ab * ranks : (ab + 1) * ranks], ab, i, j)
            acc = t if acc is None else acc + t
        o_refs[o][m] = acc.astype(o_refs[o].dtype)


def conv(idx, taps, x, x_oth, per, dtypes):
    ranks = taps.shape[1]
    return pl.pallas_call(
        conv_kernel,
        out_shape=[jax.ShapeDtypeStruct((2 * per, ranks, POS), d) for d in dtypes],
        in_specs=[SMEM] + [VMEM] * 3,
        out_specs=[VMEM] * len(dtypes),
        scratch_shapes=[pltpu.VMEM((2, 3 * x.shape[1], POS), jnp.bfloat16)],
        compiler_params=pltpu.CompilerParams(vmem_limit_bytes=16 << 20),
        name="conv_taps",
    )(idx, taps, x, x_oth)


def squares_kernel(idx_ref, c_ref, g_ref, g_oth_ref, *refs, scale):
    *bg_refs, o_ref, hi_ref, m_ref, sq_ref = refs
    x, y, core, z = idx_ref[0], idx_ref[1], idx_ref[2], idx_ref[3]
    side, width = len(bg_refs) // 2, bg_refs[0].shape[1]
    examples, ranks = c_ref.shape[0], c_ref.shape[1]
    per = examples // 2
    tensor = g_ref.shape[0] // per

    def chip(rx, ry):
        return ((x + side - rx) % side) * side + (y + side - ry) % side

    for n in range(examples):
        c = c_ref[n]
        hi_ref[n] = c.astype(jnp.bfloat16)
        hi = hi_ref[n]
        lo = (c - hi.astype(jnp.float32)).astype(jnp.bfloat16)
        both = jnp.concatenate([hi, lo], axis=0)
        src = g_ref if n < per else g_oth_ref
        g = jnp.concatenate([src[((z + tensor - t) % tensor) * per + n % per] for t in range(tensor)], axis=0)
        m = lax.dot_general(both, g, NT, preferred_element_type=jnp.float32)
        m_ref[n * ranks : (n + 1) * ranks] = (m[:ranks] + m[ranks:]).astype(jnp.bfloat16)
    m = m_ref[...]
    for half in range(2):
        for ry in range(side):
            bg = bg_refs[half * side + ry][...].reshape(side * width, -1)
            p = lax.dot_general(bg, m, NT, preferred_element_type=jnp.float32)
            p = p * p
            while p.shape[1] > 2 * ranks:
                p = p[:, : p.shape[1] // 2] + p[:, p.shape[1] // 2 :]
            p = (p + pltpu.roll(p, ranks, 1)) * scale
            for rx in range(side):
                at = (chip(rx, ry) * 2 + (core + half) % 2) * width
                sq_ref[pl.ds(pl.multiple_of(at, 8), width), :] = p[rx * width : (rx + 1) * width]
    sq = sq_ref[...].T[:ranks]
    low = ranks // (side * side)
    for b in range(side * side):
        o_ref[chip(b % side, b // side)] = sq[b * low : (b + 1) * low]


def squares(idx, c, g, g_oth, bg, bg_oth, scale):
    examples, ranks = c.shape[0], c.shape[1]
    side, width, hidden = bg[0].shape
    chips = side * side

    def kernel(*refs):
        squares_kernel(*refs, scale=scale)

    return pl.pallas_call(
        kernel,
        out_shape=jax.ShapeDtypeStruct((chips, ranks // chips, 2 * chips * width), jnp.float32),
        in_specs=[SMEM] + [VMEM] * (3 + 2 * side),
        out_specs=VMEM,
        scratch_shapes=[
            pltpu.VMEM((examples, ranks, POS), jnp.bfloat16),
            pltpu.VMEM((examples * ranks, hidden), jnp.bfloat16),
            pltpu.VMEM((2 * chips * width, 2 * ranks), jnp.float32),
        ],
        compiler_params=pltpu.CompilerParams(vmem_limit_bytes=16 << 20),
        name="squared_sums",
    )(idx, c, g, g_oth, *bg, *bg_oth)


def shift(v, axis, s):
    n = lax.axis_size(axis)
    return lax.ppermute(v, axis, [(i, (i + s) % n) for i in range(n)])


def around(v, axis):
    return [v] + [shift(v, axis, s) for s in range(1, lax.axis_size(axis))]


def body(patch_rows, out_grads, basis_a, basis_g):
    coords = [lax.axis_index(a).astype(jnp.int32) for a in ALL]
    z = coords[3]
    x = patch_rows.transpose(0, 2, 1)
    grads = out_grads.transpose(0, 2, 1)
    here, channels = x.shape[0], x.shape[1]
    tensor = lax.axis_size("z")
    per = here // tensor

    with jax.named_scope("basis_a_x"):
        own = basis_a.reshape(AB, 3, channels, -1).transpose(0, 3, 1, 2)
        own = own.reshape(AB, own.shape[1], 3 * channels)
        ba = around(own, "x")
    with jax.named_scope("basis_g_z"):
        bg = around(basis_g.T, "z")
    with jax.named_scope("exchange_grads"):
        grads, bg, ba = lax.optimization_barrier((grads, bg, ba))
        g = lax.all_to_all(grads, "z", 0, 0, tiled=True)
    with jax.named_scope("basis_a_y"):
        ba = jnp.concatenate(ba, axis=1)
        bg, give, _ = lax.optimization_barrier((bg, x, ba))
        x_oth = shift(give, "core", 1)
        ba = around(ba, "y")
    with jax.named_scope("basis_g_x"):
        bg = around(jnp.concatenate(bg, axis=1), "x")

    def parts(shifts, dtypes):
        return conv(jnp.stack([(z + s) % tensor for s in shifts]), jnp.concatenate(ba, axis=1), x, x_oth, per, dtypes)

    ba, bg = lax.optimization_barrier((ba, bg))
    with jax.named_scope("basis_g_y"):
        bg = around(jnp.stack(bg), "y")
    with jax.named_scope("coeff_parts"):
        bf16 = jnp.bfloat16
        *sent, mine = parts((2, 1, 3, 0), (bf16, bf16, bf16, jnp.float32))
        received = [shift(v, "z", s) for v, s in zip(sent, (2, 1, 3))]
    with jax.named_scope("exchange_cores"):
        g, bg, received[1] = lax.optimization_barrier((g, bg, received[1]))
        g_oth = shift(g, "core", 1)
        bg_oth = [shift(v, "core", 1) for v in bg]

    total_coeff = mine
    for r in received:
        total_coeff = total_coeff + r.astype(jnp.float32)
    examples = here * lax.axis_size(("x", "y", "core"))
    total = squares(jnp.stack(coords), total_coeff, g, g_oth, bg, bg_oth, 1.0 / examples)

    with jax.named_scope("sum_examples"):
        rows = total.reshape(-1, 1, total.shape[2])
        got = lax.all_to_all(rows, ("x", "y", "z"), 0, 0, tiled=True)
        return jnp.sum(got, axis=0)


def solution(mesh):
    tensor = mesh.shape["tensor"]
    fine = Mesh(mesh.devices.reshape(4, -1, 2, tensor), ALL)
    dp = ("x", "y", "core")
    in_specs = (P(dp, None, "z"), P(dp, None, "z"), P(None, "z", dp), P("z", dp))
    return jax.shard_map(body, mesh=fine, in_specs=in_specs, out_specs=P(ALL, None), check_vma=False)
```

```python
import jax
import jax.numpy as jnp
from jax import lax
from jax.experimental import pallas as pl
from jax.experimental.pallas import tpu as pltpu
from jax.sharding import Mesh, PartitionSpec as P

SIDE = 8
POS = SIDE * SIDE * SIDE
AB = 9
ALL = ("x", "y", "core", "z")
NT = (((1,), (1,)), ((), ()))
VMEM = pl.BlockSpec(memory_space=pltpu.VMEM)
SMEM = pl.BlockSpec(memory_space=pltpu.SMEM)


def lane_coords():
    p = lax.broadcasted_iota(jnp.int32, (1, POS), 1)
    return p // 64, (p // 8) % 8, p % 8


def shifted(y, ab, i, j):
    a, b = ab // 3 - 1, ab % 3 - 1
    s = a * 64 + b * 8
    if s == 0:
        return y
    ok = None
    for v, o in ((i, a), (j, b)):
        if o != 0:
            m = (v + o >= 0) & (v + o < SIDE)
            ok = m if ok is None else ok & m
    return jnp.where(ok, pltpu.roll(y, (-s) % POS, 1), 0.0)


def conv_kernel(idx_ref, b_ref, x_ref, x_oth_ref, *refs):
    *o_refs, xc_ref = refs
    i, j, k = lane_coords()
    h = x_ref.shape[1]
    per = o_refs[0].shape[0] // 2
    ranks = b_ref.shape[1]
    zero = jnp.zeros((), x_ref.dtype)
    b = b_ref[...].reshape(AB * ranks, 3 * h)
    for n in range(2 * per * len(o_refs)):
        o, m = n // (2 * per), n % (2 * per)
        x = (x_ref if m < per else x_oth_ref)[idx_ref[o] * per + m % per]
        xc_ref[n % 2, :h] = jnp.where(k >= 1, pltpu.roll(x, 1, 1), zero)
        xc_ref[n % 2, h : 2 * h] = x
        xc_ref[n % 2, 2 * h :] = jnp.where(k <= SIDE - 2, pltpu.roll(x, POS - 1, 1), zero)
        y = jnp.dot(b, xc_ref[n % 2], preferred_element_type=jnp.float32)
        acc = None
        for ab in range(AB):
            t = shifted(y[ab * ranks : (ab + 1) * ranks], ab, i, j)
            acc = t if acc is None else acc + t
        o_refs[o][m] = acc.astype(o_refs[o].dtype)


def conv(idx, taps, x, x_oth, per, dtypes):
    ranks = taps.shape[1]
    return pl.pallas_call(
        conv_kernel,
        out_shape=[jax.ShapeDtypeStruct((2 * per, ranks, POS), d) for d in dtypes],
        in_specs=[SMEM] + [VMEM] * 3,
        out_specs=[VMEM] * len(dtypes),
        scratch_shapes=[pltpu.VMEM((2, 3 * x.shape[1], POS), jnp.bfloat16)],
        compiler_params=pltpu.CompilerParams(vmem_limit_bytes=16 << 20),
        name="conv_taps",
    )(idx, taps, x, x_oth)


def squares_kernel(idx_ref, c_ref, g_ref, g_oth_ref, *refs, scale):
    *bg_refs, o_ref, hi_ref, m_ref, sq_ref = refs
    x, y, core, z = idx_ref[0], idx_ref[1], idx_ref[2], idx_ref[3]
    side, width = len(bg_refs) // 2, bg_refs[0].shape[1]
    examples, ranks = c_ref.shape[0], c_ref.shape[1]
    per = examples // 2
    tensor = g_ref.shape[0] // per

    def chip(rx, ry):
        return ((x + side - rx) % side) * side + (y + side - ry) % side

    for n in range(examples):
        c = c_ref[n]
        hi_ref[n] = c.astype(jnp.bfloat16)
        hi = hi_ref[n]
        lo = (c - hi.astype(jnp.float32)).astype(jnp.bfloat16)
        both = jnp.concatenate([hi, lo], axis=0)
        src = g_ref if n < per else g_oth_ref
        g = jnp.concatenate([src[((z + tensor - t) % tensor) * per + n % per] for t in range(tensor)], axis=0)
        m = lax.dot_general(both, g, NT, preferred_element_type=jnp.float32)
        m_ref[n * ranks : (n + 1) * ranks] = (m[:ranks] + m[ranks:]).astype(jnp.bfloat16)
    m = m_ref[...]
    for half in range(2):
        for ry in range(side):
            bg = bg_refs[half * side + ry][...].reshape(side * width, -1)
            p = lax.dot_general(bg, m, NT, preferred_element_type=jnp.float32)
            p = p * p
            while p.shape[1] > 2 * ranks:
                p = p[:, : p.shape[1] // 2] + p[:, p.shape[1] // 2 :]
            p = (p + pltpu.roll(p, ranks, 1)) * scale
            for rx in range(side):
                at = (chip(rx, ry) * 2 + (core + half) % 2) * width
                sq_ref[pl.ds(pl.multiple_of(at, 8), width), :] = p[rx * width : (rx + 1) * width]
    sq = sq_ref[...].T[:ranks]
    low = ranks // (side * side)
    for b in range(side * side):
        o_ref[chip(b % side, b // side)] = sq[b * low : (b + 1) * low]


def squares(idx, c, g, g_oth, bg, bg_oth, scale):
    examples, ranks = c.shape[0], c.shape[1]
    side, width, hidden = bg[0].shape
    chips = side * side

    def kernel(*refs):
        squares_kernel(*refs, scale=scale)

    return pl.pallas_call(
        kernel,
        out_shape=jax.ShapeDtypeStruct((chips, ranks // chips, 2 * chips * width), jnp.float32),
        in_specs=[SMEM] + [VMEM] * (3 + 2 * side),
        out_specs=VMEM,
        scratch_shapes=[
            pltpu.VMEM((examples, ranks, POS), jnp.bfloat16),
            pltpu.VMEM((examples * ranks, hidden), jnp.bfloat16),
            pltpu.VMEM((2 * chips * width, 2 * ranks), jnp.float32),
        ],
        compiler_params=pltpu.CompilerParams(vmem_limit_bytes=16 << 20),
        name="squared_sums",
    )(idx, c, g, g_oth, *bg, *bg_oth)


def shift(v, axis, s):
    n = lax.axis_size(axis)
    return lax.ppermute(v, axis, [(i, (i + s) % n) for i in range(n)])


def around(v, axis):
    return [v] + [shift(v, axis, s) for s in range(1, lax.axis_size(axis))]


def body(patch_rows, out_grads, basis_a, basis_g):
    coords = [lax.axis_index(a).astype(jnp.int32) for a in ALL]
    z = coords[3]
    x = patch_rows.transpose(0, 2, 1)
    grads = out_grads.transpose(0, 2, 1)
    here, channels = x.shape[0], x.shape[1]
    tensor = lax.axis_size("z")
    per = here // tensor

    with jax.named_scope("basis_a_x"):
        own = basis_a.reshape(AB, 3, channels, -1).transpose(0, 3, 1, 2)
        own = own.reshape(AB, own.shape[1], 3 * channels)
        ba = around(own, "x")
    with jax.named_scope("basis_g_z"):
        bg = around(basis_g.T, "z")
    with jax.named_scope("exchange_grads"):
        grads, bg, ba = lax.optimization_barrier((grads, bg, ba))
        g = lax.all_to_all(grads, "z", 0, 0, tiled=True)
    with jax.named_scope("basis_a_y"):
        ba = jnp.concatenate(ba, axis=1)
        bg, give, _ = lax.optimization_barrier((bg, x, ba))
        x_oth = shift(give, "core", 1)
        ba = around(ba, "y")
    with jax.named_scope("basis_g_x"):
        bg = around(jnp.concatenate(bg, axis=1), "x")

    def parts(shifts, dtypes):
        return conv(jnp.stack([(z + s) % tensor for s in shifts]), jnp.concatenate(ba, axis=1), x, x_oth, per, dtypes)

    ba, bg = lax.optimization_barrier((ba, bg))
    with jax.named_scope("basis_g_y"):
        bg = around(jnp.stack(bg), "y")
    with jax.named_scope("coeff_parts"):
        bf16 = jnp.bfloat16
        *sent, mine = parts((2, 1, 3, 0), (bf16, bf16, bf16, jnp.float32))
        received = [shift(v, "z", s) for v, s in zip(sent, (2, 1, 3))]
    with jax.named_scope("exchange_cores"):
        g, bg, _ = lax.optimization_barrier((g, bg, sent[0]))
        g_oth = shift(g, "core", 1)
        first = shift(bg[0], "core", 1)
        rest, first = lax.optimization_barrier((bg[1:], first))
        bg_oth = [first] + [shift(v, "core", 1) for v in rest]

    total_coeff = mine
    for r in received:
        total_coeff = total_coeff + r.astype(jnp.float32)
    examples = here * lax.axis_size(("x", "y", "core"))
    total = squares(jnp.stack(coords), total_coeff, g, g_oth, bg, bg_oth, 1.0 / examples)

    with jax.named_scope("sum_examples"):
        rows = total.reshape(-1, 1, total.shape[2])
        got = lax.all_to_all(rows, ("x", "y", "z"), 0, 0, tiled=True)
        return jnp.sum(got, axis=0)


def solution(mesh):
    tensor = mesh.shape["tensor"]
    fine = Mesh(mesh.devices.reshape(4, -1, 2, tensor), ALL)
    dp = ("x", "y", "core")
    in_specs = (P(dp, None, "z"), P(dp, None, "z"), P(None, "z", dp), P("z", dp))
    return jax.shard_map(body, mesh=fine, in_specs=in_specs, out_specs=P(ALL, None), check_vma=False)
```

```python
import jax
import jax.numpy as jnp
from jax import lax
from jax.experimental import pallas as pl
from jax.experimental.pallas import tpu as pltpu
from jax.sharding import Mesh, PartitionSpec as P

SIDE = 8
POS = SIDE * SIDE * SIDE
AB = 9
ALL = ("x", "y", "core", "z")
NT = (((1,), (1,)), ((), ()))
VMEM = pl.BlockSpec(memory_space=pltpu.VMEM)
SMEM = pl.BlockSpec(memory_space=pltpu.SMEM)


def lane_coords():
    p = lax.broadcasted_iota(jnp.int32, (1, POS), 1)
    return p // 64, (p // 8) % 8, p % 8


def shifted(y, ab, i, j):
    a, b = ab // 3 - 1, ab % 3 - 1
    s = a * 64 + b * 8
    if s == 0:
        return y
    ok = None
    for v, o in ((i, a), (j, b)):
        if o != 0:
            m = (v + o >= 0) & (v + o < SIDE)
            ok = m if ok is None else ok & m
    return jnp.where(ok, pltpu.roll(y, (-s) % POS, 1), 0.0)


def conv_kernel(idx_ref, b_ref, x_ref, x_oth_ref, *refs):
    *o_refs, xc_ref = refs
    i, j, k = lane_coords()
    h = x_ref.shape[1]
    per = o_refs[0].shape[0] // 2
    ranks = b_ref.shape[1]
    zero = jnp.zeros((), x_ref.dtype)
    b = b_ref[...].reshape(AB * ranks, 3 * h)
    for n in range(2 * per * len(o_refs)):
        o, m = n // (2 * per), n % (2 * per)
        x = (x_ref if m < per else x_oth_ref)[idx_ref[o] * per + m % per]
        xc_ref[n % 2, :h] = jnp.where(k >= 1, pltpu.roll(x, 1, 1), zero)
        xc_ref[n % 2, h : 2 * h] = x
        xc_ref[n % 2, 2 * h :] = jnp.where(k <= SIDE - 2, pltpu.roll(x, POS - 1, 1), zero)
        y = jnp.dot(b, xc_ref[n % 2], preferred_element_type=jnp.float32)
        acc = None
        for ab in range(AB):
            t = shifted(y[ab * ranks : (ab + 1) * ranks], ab, i, j)
            acc = t if acc is None else acc + t
        o_refs[o][m] = acc.astype(o_refs[o].dtype)


def conv(idx, taps, x, x_oth, per, dtypes):
    ranks = taps.shape[1]
    return pl.pallas_call(
        conv_kernel,
        out_shape=[jax.ShapeDtypeStruct((2 * per, ranks, POS), d) for d in dtypes],
        in_specs=[SMEM] + [VMEM] * 3,
        out_specs=[VMEM] * len(dtypes),
        scratch_shapes=[pltpu.VMEM((2, 3 * x.shape[1], POS), jnp.bfloat16)],
        compiler_params=pltpu.CompilerParams(vmem_limit_bytes=16 << 20),
        name="conv_taps",
    )(idx, taps, x, x_oth)


def squares_kernel(idx_ref, c_ref, g_ref, g_oth_ref, *refs, scale):
    *bg_refs, o_ref, hi_ref, m_ref, sq_ref = refs
    x, y, core, z = idx_ref[0], idx_ref[1], idx_ref[2], idx_ref[3]
    side, width = len(bg_refs) // 2, bg_refs[0].shape[1]
    examples, ranks = c_ref.shape[0], c_ref.shape[1]
    per = examples // 2
    tensor = g_ref.shape[0] // per

    def chip(rx, ry):
        return ((x + side - rx) % side) * side + (y + side - ry) % side

    for n in range(examples):
        c = c_ref[n]
        hi_ref[n] = c.astype(jnp.bfloat16)
        hi = hi_ref[n]
        lo = (c - hi.astype(jnp.float32)).astype(jnp.bfloat16)
        both = jnp.concatenate([hi, lo], axis=0)
        src = g_ref if n < per else g_oth_ref
        g = jnp.concatenate([src[((z + tensor - t) % tensor) * per + n % per] for t in range(tensor)], axis=0)
        m = lax.dot_general(both, g, NT, preferred_element_type=jnp.float32)
        m_ref[n * ranks : (n + 1) * ranks] = (m[:ranks] + m[ranks:]).astype(jnp.bfloat16)
    m = m_ref[...]
    for half in range(2):
        for ry in range(side):
            bg = bg_refs[half * side + ry][...].reshape(side * width, -1)
            p = lax.dot_general(bg, m, NT, preferred_element_type=jnp.float32)
            p = p * p
            while p.shape[1] > 2 * ranks:
                p = p[:, : p.shape[1] // 2] + p[:, p.shape[1] // 2 :]
            p = (p + pltpu.roll(p, ranks, 1)) * scale
            for rx in range(side):
                at = (chip(rx, ry) * 2 + (core + half) % 2) * width
                sq_ref[pl.ds(pl.multiple_of(at, 8), width), :] = p[rx * width : (rx + 1) * width]
    sq = sq_ref[...].T[:ranks]
    low = ranks // (side * side)
    for b in range(side * side):
        o_ref[chip(b % side, b // side)] = sq[b * low : (b + 1) * low]


def squares(idx, c, g, g_oth, bg, bg_oth, scale):
    examples, ranks = c.shape[0], c.shape[1]
    side, width, hidden = bg[0].shape
    chips = side * side

    def kernel(*refs):
        squares_kernel(*refs, scale=scale)

    return pl.pallas_call(
        kernel,
        out_shape=jax.ShapeDtypeStruct((chips, ranks // chips, 2 * chips * width), jnp.float32),
        in_specs=[SMEM] + [VMEM] * (3 + 2 * side),
        out_specs=VMEM,
        scratch_shapes=[
            pltpu.VMEM((examples, ranks, POS), jnp.bfloat16),
            pltpu.VMEM((examples * ranks, hidden), jnp.bfloat16),
            pltpu.VMEM((2 * chips * width, 2 * ranks), jnp.float32),
        ],
        compiler_params=pltpu.CompilerParams(vmem_limit_bytes=16 << 20),
        name="squared_sums",
    )(idx, c, g, g_oth, *bg, *bg_oth)


def shift(v, axis, s):
    n = lax.axis_size(axis)
    return lax.ppermute(v, axis, [(i, (i + s) % n) for i in range(n)])


def around(v, axis):
    return [v] + [shift(v, axis, s) for s in range(1, lax.axis_size(axis))]


def body(patch_rows, out_grads, basis_a, basis_g):
    coords = [lax.axis_index(a).astype(jnp.int32) for a in ALL]
    z = coords[3]
    x = patch_rows.transpose(0, 2, 1)
    grads = out_grads.transpose(0, 2, 1)
    here, channels = x.shape[0], x.shape[1]
    tensor = lax.axis_size("z")
    per = here // tensor

    with jax.named_scope("basis_a_x"):
        own = basis_a.reshape(AB, 3, channels, -1).transpose(0, 3, 1, 2)
        own = own.reshape(AB, own.shape[1], 3 * channels)
        ba = around(own, "x")
    with jax.named_scope("basis_g_x"):
        bg = around(basis_g.T, "x")

    ba, bg = lax.optimization_barrier((ba, bg))
    with jax.named_scope("basis_a_y"):
        ba = jnp.concatenate(ba, axis=1)
        bg, ba = lax.optimization_barrier((bg, ba))
        ba = around(ba, "y")
    with jax.named_scope("basis_g_z"):
        bg = around(jnp.stack(bg), "z")

    ba, bg, grads, give = lax.optimization_barrier((ba, bg, grads, x))
    with jax.named_scope("exchange_inputs"):
        x_oth = shift(give, "core", 1)
    with jax.named_scope("exchange_grads"):
        g = lax.all_to_all(grads, "z", 0, 0, tiled=True)
    with jax.named_scope("basis_g_y"):
        bg = around(jnp.concatenate(bg, axis=2), "y")
    with jax.named_scope("coeff_parts"):
        bf16 = jnp.bfloat16
        shifts = (2, 1, 3, 0)
        taps, blocks = jnp.concatenate(ba, axis=1), jnp.stack([(z + s) % tensor for s in shifts])
        *sent, mine = conv(blocks, taps, x, x_oth, per, (bf16, bf16, bf16, jnp.float32))
        received = [shift(v, "z", s) for v, s in zip(sent, shifts)]
    with jax.named_scope("exchange_cores"):
        g, bg, _ = lax.optimization_barrier((g, bg, sent[0]))
        g_oth = shift(g, "core", 1)
        first = shift(bg[0], "core", 1)
        rest, first = lax.optimization_barrier((bg[1:], first))
        bg_oth = [first] + [shift(v, "core", 1) for v in rest]

    total_coeff = mine
    for r in received:
        total_coeff = total_coeff + r.astype(jnp.float32)
    examples = here * lax.axis_size(("x", "y", "core"))
    total = squares(jnp.stack(coords), total_coeff, g, g_oth, bg, bg_oth, 1.0 / examples)

    with jax.named_scope("sum_examples"):
        rows = total.reshape(-1, 1, total.shape[2])
        got = lax.all_to_all(rows, ("x", "y", "z"), 0, 0, tiled=True)
        return jnp.sum(got, axis=0)


def solution(mesh):
    tensor = mesh.shape["tensor"]
    fine = Mesh(mesh.devices.reshape(4, -1, 2, tensor), ALL)
    dp = ("x", "y", "core")
    in_specs = (P(dp, None, "z"), P(dp, None, "z"), P(None, "z", dp), P("z", dp))
    return jax.shard_map(body, mesh=fine, in_specs=in_specs, out_specs=P(ALL, None), check_vma=False)
```

```python
import jax
import jax.numpy as jnp
from jax import lax
from jax.experimental import pallas as pl
from jax.experimental.pallas import tpu as pltpu
from jax.sharding import Mesh, PartitionSpec as P

SIDE = 8
POS = SIDE * SIDE * SIDE
AB = 9
ALL = ("x", "y", "core", "z")
NT = (((1,), (1,)), ((), ()))
VMEM = pl.BlockSpec(memory_space=pltpu.VMEM)
SMEM = pl.BlockSpec(memory_space=pltpu.SMEM)


def lane_coords():
    p = lax.broadcasted_iota(jnp.int32, (1, POS), 1)
    return p // 64, (p // 8) % 8, p % 8


def shifted(y, ab, i, j):
    a, b = ab // 3 - 1, ab % 3 - 1
    s = a * 64 + b * 8
    if s == 0:
        return y
    ok = None
    for v, o in ((i, a), (j, b)):
        if o != 0:
            m = (v + o >= 0) & (v + o < SIDE)
            ok = m if ok is None else ok & m
    return jnp.where(ok, pltpu.roll(y, (-s) % POS, 1), 0.0)


def conv_kernel(idx_ref, b_ref, x_ref, x_oth_ref, o_ref, rest_ref, xc_ref):
    i, j, k = lane_coords()
    h = x_ref.shape[1]
    blocks, per, ranks = o_ref.shape[0], o_ref.shape[1] // 2, b_ref.shape[1]
    zero = jnp.zeros((), x_ref.dtype)
    b = b_ref[...].reshape(AB * ranks, 3 * h)
    for n in range(2 * per * blocks):
        o, m = n // (2 * per), n % (2 * per)
        block = (idx_ref[0] + o) % blocks
        x = (x_ref if m < per else x_oth_ref)[block * per + m % per]
        xc_ref[n % 2, :h] = jnp.where(k >= 1, pltpu.roll(x, 1, 1), zero)
        xc_ref[n % 2, h : 2 * h] = x
        xc_ref[n % 2, 2 * h :] = jnp.where(k <= SIDE - 2, pltpu.roll(x, POS - 1, 1), zero)
        y = jnp.dot(b, xc_ref[n % 2], preferred_element_type=jnp.float32)
        acc = None
        for ab in range(AB):
            t = shifted(y[ab * ranks : (ab + 1) * ranks], ab, i, j)
            acc = t if acc is None else acc + t
        o_ref[block, m] = acc.astype(o_ref.dtype)
        if o == 0:
            rest_ref[m] = acc - o_ref[block, m].astype(jnp.float32)


def conv(z, taps, x, x_oth, blocks):
    ranks, per = taps.shape[1], x.shape[0] // blocks
    return pl.pallas_call(
        conv_kernel,
        out_shape=[
            jax.ShapeDtypeStruct((blocks, 2 * per, ranks, POS), jnp.bfloat16),
            jax.ShapeDtypeStruct((2 * per, ranks, POS), jnp.float32),
        ],
        in_specs=[SMEM] + [VMEM] * 3,
        out_specs=[VMEM] * 2,
        scratch_shapes=[pltpu.VMEM((2, 3 * x.shape[1], POS), jnp.bfloat16)],
        compiler_params=pltpu.CompilerParams(vmem_limit_bytes=16 << 20),
        name="conv_taps",
    )(z, taps, x, x_oth)


def squares_kernel(idx_ref, c_ref, rest_ref, g_ref, g_oth_ref, *refs, scale):
    *bg_refs, o_ref, hi_ref, m_ref, sq_ref = refs
    x, y, core = idx_ref[0], idx_ref[1], idx_ref[2]
    side, width = len(bg_refs) // 2, bg_refs[0].shape[1]
    tensor, examples, ranks = c_ref.shape[0], c_ref.shape[1], c_ref.shape[2]
    per = examples // 2

    def chip(rx, ry):
        return ((x + side - rx) % side) * side + (y + side - ry) % side

    low_half = lax.broadcasted_iota(jnp.int32, (1, 2 * ranks), 1) < ranks
    pair = None
    for n in range(examples):
        c = rest_ref[n]
        for t in range(tensor):
            c = c + c_ref[t, n].astype(jnp.float32)
        hi_ref[n] = c.astype(jnp.bfloat16)
        hi = hi_ref[n]
        lo = (c - hi.astype(jnp.float32)).astype(jnp.bfloat16)
        both = jnp.concatenate([hi, lo], axis=0)
        src = g_ref if n < per else g_oth_ref
        g = jnp.concatenate([src[t * per + n % per] for t in range(tensor)], axis=0)
        m = lax.dot_general(g, both, NT, preferred_element_type=jnp.float32)
        m = m + pltpu.roll(m, ranks, 1)
        if n % 2 == 0:
            pair = m
        else:
            m_ref[:, (n - 1) * ranks : (n + 1) * ranks] = jnp.where(low_half, pair, m).astype(jnp.bfloat16)
    m = m_ref[...]
    for half in range(2):
        for ry in range(side):
            bg = bg_refs[half * side + ry][...].reshape(side * width, -1)
            p = jnp.dot(bg, m, preferred_element_type=jnp.float32)
            p = p * p
            while p.shape[1] > 2 * ranks:
                p = p[:, : p.shape[1] // 2] + p[:, p.shape[1] // 2 :]
            p = (p + pltpu.roll(p, ranks, 1)) * scale
            for rx in range(side):
                at = (chip(rx, ry) * 2 + (core + half) % 2) * width
                sq_ref[pl.ds(pl.multiple_of(at, 8), width), :] = p[rx * width : (rx + 1) * width]
    sq = sq_ref[...].T[:ranks]
    low = ranks // (side * side)
    for b in range(side * side):
        o_ref[chip(b % side, b // side)] = sq[b * low : (b + 1) * low]


def squares(idx, c, rest, g, g_oth, bg, bg_oth, scale):
    examples, ranks = rest.shape[0], rest.shape[1]
    side, width, hidden = bg[0].shape
    chips = side * side

    def kernel(*refs):
        squares_kernel(*refs, scale=scale)

    return pl.pallas_call(
        kernel,
        out_shape=jax.ShapeDtypeStruct((chips, ranks // chips, 2 * chips * width), jnp.float32),
        in_specs=[SMEM] + [VMEM] * (4 + 2 * side),
        out_specs=VMEM,
        scratch_shapes=[
            pltpu.VMEM((examples, ranks, POS), jnp.bfloat16),
            pltpu.VMEM((hidden, examples * ranks), jnp.bfloat16),
            pltpu.VMEM((2 * chips * width, 2 * ranks), jnp.float32),
        ],
        compiler_params=pltpu.CompilerParams(vmem_limit_bytes=16 << 20),
        name="squared_sums",
    )(idx, c, rest, g, g_oth, *bg, *bg_oth)


def shift(v, axis, s):
    n = lax.axis_size(axis)
    return lax.ppermute(v, axis, [(i, (i + s) % n) for i in range(n)])


def around(v, axis):
    return [v] + [shift(v, axis, s) for s in range(1, lax.axis_size(axis))]


def body(patch_rows, out_grads, basis_a, basis_g):
    coords = [lax.axis_index(a).astype(jnp.int32) for a in ALL]
    z = coords[3]
    x = patch_rows.transpose(0, 2, 1)
    grads = out_grads.transpose(0, 2, 1)
    here, channels = x.shape[0], x.shape[1]
    tensor = lax.axis_size("z")
    per = here // tensor

    with jax.named_scope("basis_a_x"):
        own = basis_a.reshape(AB, 3, channels, -1).transpose(0, 3, 1, 2)
        own = own.reshape(AB, own.shape[1], 3 * channels)
        ba = around(own, "x")
    with jax.named_scope("basis_g_z"):
        bg = basis_g.T
        bg = lax.all_to_all(jnp.broadcast_to(bg[None], (tensor, *bg.shape)), "z", 0, 0, tiled=True)
    with jax.named_scope("exchange_grads"):
        grads, bg, ba = lax.optimization_barrier((grads, bg, ba))
        g = lax.all_to_all(grads, "z", 0, 0, tiled=True)
    with jax.named_scope("basis_a_y"):
        ba = jnp.concatenate(ba, axis=1)
        bg, give, _ = lax.optimization_barrier((bg, x, ba))
        x_oth = shift(give, "core", 1)
        ba = around(ba, "y")
    with jax.named_scope("basis_g_x"):
        bg = around(jnp.concatenate(list(bg), axis=1), "x")

    ba, bg = lax.optimization_barrier((ba, bg))
    with jax.named_scope("basis_g_y"):
        bg = around(jnp.stack(bg), "y")
    with jax.named_scope("coeff_parts"):
        sent, rest = conv(z.reshape(1), jnp.concatenate(ba, axis=1), x, x_oth, tensor)
        received = lax.all_to_all(sent, "z", 0, 0, tiled=True)
    with jax.named_scope("exchange_cores"):
        g, bg, _ = lax.optimization_barrier((g, bg, sent))
        g_oth = shift(g, "core", 1)
        first = shift(bg[0], "core", 1)
        later, first = lax.optimization_barrier((bg[1:], first))
        bg_oth = [first] + [shift(v, "core", 1) for v in later]

    examples = here * lax.axis_size(("x", "y", "core"))
    total = squares(jnp.stack(coords), received, rest, g, g_oth, bg, bg_oth, 1.0 / examples)

    with jax.named_scope("sum_examples"):
        rows = total.reshape(-1, 1, total.shape[2])
        got = lax.all_to_all(rows, ("x", "y", "z"), 0, 0, tiled=True)
        return jnp.sum(got, axis=0)


def solution(mesh):
    tensor = mesh.shape["tensor"]
    fine = Mesh(mesh.devices.reshape(4, -1, 2, tensor), ALL)
    dp = ("x", "y", "core")
    in_specs = (P(dp, None, "z"), P(dp, None, "z"), P(None, "z", dp), P("z", dp))
    return jax.shard_map(body, mesh=fine, in_specs=in_specs, out_specs=P(ALL, None), check_vma=False)
```

```python
import jax
import jax.numpy as jnp
from jax import lax
from jax.experimental import pallas as pl
from jax.experimental.pallas import tpu as pltpu
from jax.sharding import Mesh, PartitionSpec as P

SIDE = 8
POS = SIDE * SIDE * SIDE
AB = 9
ALL = ("x", "y", "core", "z")
NT = (((1,), (1,)), ((), ()))
VMEM = pl.BlockSpec(memory_space=pltpu.VMEM)
SMEM = pl.BlockSpec(memory_space=pltpu.SMEM)


def lane_coords():
    p = lax.broadcasted_iota(jnp.int32, (1, POS), 1)
    return p // 64, (p // 8) % 8, p % 8


def shifted(y, ab, i, j):
    a, b = ab // 3 - 1, ab % 3 - 1
    s = a * 64 + b * 8
    if s == 0:
        return y
    ok = None
    for v, o in ((i, a), (j, b)):
        if o != 0:
            m = (v + o >= 0) & (v + o < SIDE)
            ok = m if ok is None else ok & m
    return jnp.where(ok, pltpu.roll(y, (-s) % POS, 1), 0.0)


def conv_kernel(idx_ref, b_ref, x_ref, x_oth_ref, *refs):
    *o_refs, xc_ref = refs
    i, j, k = lane_coords()
    h = x_ref.shape[1]
    per = o_refs[0].shape[0] // 2
    ranks = b_ref.shape[1]
    zero = jnp.zeros((), x_ref.dtype)
    b = b_ref[...].reshape(AB * ranks, 3 * h)
    for n in range(2 * per * len(o_refs)):
        o, m = n // (2 * per), n % (2 * per)
        x = (x_ref if m < per else x_oth_ref)[idx_ref[o] * per + m % per]
        xc_ref[n % 2, :h] = jnp.where(k >= 1, pltpu.roll(x, 1, 1), zero)
        xc_ref[n % 2, h : 2 * h] = x
        xc_ref[n % 2, 2 * h :] = jnp.where(k <= SIDE - 2, pltpu.roll(x, POS - 1, 1), zero)
        y = jnp.dot(b, xc_ref[n % 2], preferred_element_type=jnp.float32)
        acc = None
        for ab in range(AB):
            t = shifted(y[ab * ranks : (ab + 1) * ranks], ab, i, j)
            acc = t if acc is None else acc + t
        o_refs[o][m] = acc.astype(o_refs[o].dtype)


def conv(idx, taps, x, x_oth, per, dtypes):
    ranks = taps.shape[1]
    return pl.pallas_call(
        conv_kernel,
        out_shape=[jax.ShapeDtypeStruct((2 * per, ranks, POS), d) for d in dtypes],
        in_specs=[SMEM] + [VMEM] * 3,
        out_specs=[VMEM] * len(dtypes),
        scratch_shapes=[pltpu.VMEM((2, 3 * x.shape[1], POS), jnp.bfloat16)],
        compiler_params=pltpu.CompilerParams(vmem_limit_bytes=16 << 20),
        name="conv_taps",
    )(idx, taps, x, x_oth)


def squares_kernel(idx_ref, own_ref, r1_ref, r2_ref, r3_ref, g_ref, g_oth_ref, *refs, scale):
    *bg_refs, o_ref, hi_ref, m_ref, sq_ref = refs
    x, y, core = idx_ref[0], idx_ref[1], idx_ref[2]
    side, width = len(bg_refs) // 2, bg_refs[0].shape[1]
    examples, ranks = own_ref.shape[0], own_ref.shape[1]
    per = examples // 2
    tensor = g_ref.shape[0] // per

    def chip(rx, ry):
        return ((x + side - rx) % side) * side + (y + side - ry) % side

    low_half = lax.broadcasted_iota(jnp.int32, (1, 2 * ranks), 1) < ranks
    pair = None
    for n in range(examples):
        c = own_ref[n]
        for r in (r1_ref, r2_ref, r3_ref):
            c = c + r[n].astype(jnp.float32)
        hi_ref[n] = c.astype(jnp.bfloat16)
        hi = hi_ref[n]
        lo = (c - hi.astype(jnp.float32)).astype(jnp.bfloat16)
        both = jnp.concatenate([hi, lo], axis=0)
        src = g_ref if n < per else g_oth_ref
        g = jnp.concatenate([src[t * per + n % per] for t in range(tensor)], axis=0)
        m = lax.dot_general(g, both, NT, preferred_element_type=jnp.float32)
        m = m + pltpu.roll(m, ranks, 1)
        if n % 2 == 0:
            pair = m
        else:
            m_ref[:, (n - 1) * ranks : (n + 1) * ranks] = jnp.where(low_half, pair, m).astype(jnp.bfloat16)
    m = m_ref[...]
    for half in range(2):
        for ry in range(side):
            bg = bg_refs[half * side + ry][...].reshape(side * width, -1)
            p = jnp.dot(bg, m, preferred_element_type=jnp.float32)
            p = p * p
            while p.shape[1] > 2 * ranks:
                p = p[:, : p.shape[1] // 2] + p[:, p.shape[1] // 2 :]
            p = (p + pltpu.roll(p, ranks, 1)) * scale
            for rx in range(side):
                at = (chip(rx, ry) * 2 + (core + half) % 2) * width
                sq_ref[pl.ds(pl.multiple_of(at, 8), width), :] = p[rx * width : (rx + 1) * width]
    sq = sq_ref[...].T[:ranks]
    low = ranks // (side * side)
    for b in range(side * side):
        o_ref[chip(b % side, b // side)] = sq[b * low : (b + 1) * low]


def squares(idx, own, received, g, g_oth, bg, bg_oth, scale):
    examples, ranks = own.shape[0], own.shape[1]
    side, width, hidden = bg[0].shape
    chips = side * side

    def kernel(*refs):
        squares_kernel(*refs, scale=scale)

    return pl.pallas_call(
        kernel,
        out_shape=jax.ShapeDtypeStruct((chips, ranks // chips, 2 * chips * width), jnp.float32),
        in_specs=[SMEM] + [VMEM] * (6 + 2 * side),
        out_specs=VMEM,
        scratch_shapes=[
            pltpu.VMEM((examples, ranks, POS), jnp.bfloat16),
            pltpu.VMEM((hidden, examples * ranks), jnp.bfloat16),
            pltpu.VMEM((2 * chips * width, 2 * ranks), jnp.float32),
        ],
        compiler_params=pltpu.CompilerParams(vmem_limit_bytes=16 << 20),
        name="squared_sums",
    )(idx, own, *received, g, g_oth, *bg, *bg_oth)


def shift(v, axis, s):
    n = lax.axis_size(axis)
    return lax.ppermute(v, axis, [(i, (i + s) % n) for i in range(n)])


def around(v, axis):
    return [v] + [shift(v, axis, s) for s in range(1, lax.axis_size(axis))]


def body(patch_rows, out_grads, basis_a, basis_g):
    coords = [lax.axis_index(a).astype(jnp.int32) for a in ALL]
    z = coords[3]
    x = patch_rows.transpose(0, 2, 1)
    grads = out_grads.transpose(0, 2, 1)
    here, channels = x.shape[0], x.shape[1]
    tensor = lax.axis_size("z")
    per = here // tensor

    with jax.named_scope("basis_a_x"):
        own = basis_a.reshape(AB, 3, channels, -1).transpose(0, 3, 1, 2)
        own = own.reshape(AB, own.shape[1], 3 * channels)
        ba = around(own, "x")
    with jax.named_scope("basis_g_z"):
        bg = basis_g.T
        bg = lax.all_to_all(jnp.broadcast_to(bg[None], (tensor, *bg.shape)), "z", 0, 0, tiled=True)
    with jax.named_scope("exchange_grads"):
        grads, bg, ba = lax.optimization_barrier((grads, bg, ba))
        g = lax.all_to_all(grads, "z", 0, 0, tiled=True)
    with jax.named_scope("basis_a_y"):
        ba = jnp.concatenate(ba, axis=1)
        bg, give, _ = lax.optimization_barrier((bg, x, ba))
        x_oth = shift(give, "core", 1)
        ba = around(ba, "y")
    with jax.named_scope("basis_g_x"):
        bg = around(jnp.concatenate(list(bg), axis=1), "x")

    ba, bg = lax.optimization_barrier((ba, bg))
    with jax.named_scope("basis_g_y"):
        bg = around(jnp.stack(bg), "y")
    with jax.named_scope("coeff_parts"):
        bf16 = jnp.bfloat16
        blocks = [(z + s) % tensor for s in (2, 1, 3, 0)]
        far, near = conv(jnp.stack(blocks[:2]), jnp.concatenate(ba, axis=1), x, x_oth, per, (bf16, bf16))
        received = [shift(far, "z", 2), shift(near, "z", 1)]
        ba, blocks, _ = lax.optimization_barrier((ba, blocks, far))
        last, mine = conv(jnp.stack(blocks[2:]), jnp.concatenate(ba, axis=1), x, x_oth, per, (bf16, jnp.float32))
    with jax.named_scope("exchange_cores"):
        g, bg, received, mine = lax.optimization_barrier((g, bg, received, mine))
        g_oth = shift(g, "core", 1)
        bg_oth = [shift(v, "core", 1) for v in bg]
    received.append(shift(last, "z", 3))

    examples = here * lax.axis_size(("x", "y", "core"))
    total = squares(jnp.stack(coords), mine, received, g, g_oth, bg, bg_oth, 1.0 / examples)

    with jax.named_scope("sum_examples"):
        rows = total.reshape(-1, 1, total.shape[2])
        got = lax.all_to_all(rows, ("x", "y", "z"), 0, 0, tiled=True)
        return jnp.sum(got, axis=0)


def solution(mesh):
    tensor = mesh.shape["tensor"]
    fine = Mesh(mesh.devices.reshape(4, -1, 2, tensor), ALL)
    dp = ("x", "y", "core")
    in_specs = (P(dp, None, "z"), P(dp, None, "z"), P(None, "z", dp), P("z", dp))
    return jax.shard_map(body, mesh=fine, in_specs=in_specs, out_specs=P(ALL, None), check_vma=False)
```

```python
import jax
import jax.numpy as jnp
from jax import lax
from jax.experimental import pallas as pl
from jax.experimental.pallas import tpu as pltpu
from jax.sharding import Mesh, PartitionSpec as P

SIDE = 8
POS = SIDE * SIDE * SIDE
AB = 9
ALL = ("x", "y", "core", "z")
NT = (((1,), (1,)), ((), ()))
VMEM = pl.BlockSpec(memory_space=pltpu.VMEM)
SMEM = pl.BlockSpec(memory_space=pltpu.SMEM)


def lane_coords():
    p = lax.broadcasted_iota(jnp.int32, (1, POS), 1)
    return p // 64, (p // 8) % 8, p % 8


def shifted(y, ab, i, j):
    a, b = ab // 3 - 1, ab % 3 - 1
    s = a * 64 + b * 8
    if s == 0:
        return y
    ok = None
    for v, o in ((i, a), (j, b)):
        if o != 0:
            m = (v + o >= 0) & (v + o < SIDE)
            ok = m if ok is None else ok & m
    return jnp.where(ok, pltpu.roll(y, (-s) % POS, 1), 0.0)


def conv_kernel(idx_ref, b_ref, x_ref, x_oth_ref, *refs):
    *o_refs, xc_ref = refs
    i, j, k = lane_coords()
    h = x_ref.shape[1]
    per = o_refs[0].shape[0] // 2
    ranks = b_ref.shape[1]
    zero = jnp.zeros((), x_ref.dtype)
    b = b_ref[...].reshape(AB * ranks, 3 * h)
    for n in range(2 * per * len(o_refs)):
        o, m = n // (2 * per), n % (2 * per)
        x = (x_ref if m < per else x_oth_ref)[idx_ref[o] * per + m % per]
        xc_ref[n % 2, :h] = jnp.where(k >= 1, pltpu.roll(x, 1, 1), zero)
        xc_ref[n % 2, h : 2 * h] = x
        xc_ref[n % 2, 2 * h :] = jnp.where(k <= SIDE - 2, pltpu.roll(x, POS - 1, 1), zero)
        y = jnp.dot(b, xc_ref[n % 2], preferred_element_type=jnp.float32)
        acc = None
        for ab in range(AB):
            t = shifted(y[ab * ranks : (ab + 1) * ranks], ab, i, j)
            acc = t if acc is None else acc + t
        o_refs[o][m] = acc.astype(o_refs[o].dtype)


def conv(idx, taps, x, x_oth, per, dtypes):
    ranks = taps.shape[1]
    return pl.pallas_call(
        conv_kernel,
        out_shape=[jax.ShapeDtypeStruct((2 * per, ranks, POS), d) for d in dtypes],
        in_specs=[SMEM] + [VMEM] * 3,
        out_specs=[VMEM] * len(dtypes),
        scratch_shapes=[pltpu.VMEM((2, 3 * x.shape[1], POS), jnp.bfloat16)],
        compiler_params=pltpu.CompilerParams(vmem_limit_bytes=52 << 20),
        name="conv_taps",
    )(idx, taps, x, x_oth)


def squares_kernel(idx_ref, own_ref, r1_ref, r2_ref, r3_ref, g_ref, g_oth_ref, *refs, scale):
    *bg_refs, o_ref, hi_ref, m_ref, sq_ref = refs
    x, y, core = idx_ref[0], idx_ref[1], idx_ref[2]
    side, width = len(bg_refs) // 2, bg_refs[0].shape[1]
    examples, ranks = own_ref.shape[0], own_ref.shape[1]
    per = examples // 2
    tensor = g_ref.shape[0] // per

    def chip(rx, ry):
        return ((x + side - rx) % side) * side + (y + side - ry) % side

    low_half = lax.broadcasted_iota(jnp.int32, (1, 2 * ranks), 1) < ranks
    pair = None
    for n in range(examples):
        c = own_ref[n]
        for r in (r1_ref, r2_ref, r3_ref):
            c = c + r[n].astype(jnp.float32)
        hi_ref[n] = c.astype(jnp.bfloat16)
        hi = hi_ref[n]
        lo = (c - hi.astype(jnp.float32)).astype(jnp.bfloat16)
        both = jnp.concatenate([hi, lo], axis=0)
        src = g_ref if n < per else g_oth_ref
        g = jnp.concatenate([src[t * per + n % per] for t in range(tensor)], axis=0)
        m = lax.dot_general(g, both, NT, preferred_element_type=jnp.float32)
        m = m + pltpu.roll(m, ranks, 1)
        if n % 2 == 0:
            pair = m
        else:
            m_ref[:, (n - 1) * ranks : (n + 1) * ranks] = jnp.where(low_half, pair, m).astype(jnp.bfloat16)
    m = m_ref[...]
    for half in range(2):
        for ry in range(side):
            bg = bg_refs[half * side + ry][...].reshape(side * width, -1)
            p = jnp.dot(bg, m, preferred_element_type=jnp.float32)
            p = p * p
            while p.shape[1] > 2 * ranks:
                p = p[:, : p.shape[1] // 2] + p[:, p.shape[1] // 2 :]
            p = (p + pltpu.roll(p, ranks, 1)) * scale
            for rx in range(side):
                at = (chip(rx, ry) * 2 + (core + half) % 2) * width
                sq_ref[pl.ds(pl.multiple_of(at, 8), width), :] = p[rx * width : (rx + 1) * width]
    sq = sq_ref[...].T[:ranks]
    low = ranks // (side * side)
    for b in range(side * side):
        o_ref[chip(b % side, b // side)] = sq[b * low : (b + 1) * low]


def squares(idx, own, received, g, g_oth, bg, bg_oth, scale):
    examples, ranks = own.shape[0], own.shape[1]
    side, width, hidden = bg[0].shape
    chips = side * side

    def kernel(*refs):
        squares_kernel(*refs, scale=scale)

    return pl.pallas_call(
        kernel,
        out_shape=jax.ShapeDtypeStruct((chips, ranks // chips, 2 * chips * width), jnp.float32),
        in_specs=[SMEM] + [VMEM] * (6 + 2 * side),
        out_specs=VMEM,
        scratch_shapes=[
            pltpu.VMEM((examples, ranks, POS), jnp.bfloat16),
            pltpu.VMEM((hidden, examples * ranks), jnp.bfloat16),
            pltpu.VMEM((2 * chips * width, 2 * ranks), jnp.float32),
        ],
        compiler_params=pltpu.CompilerParams(vmem_limit_bytes=52 << 20),
        name="squared_sums",
    )(idx, own, *received, g, g_oth, *bg, *bg_oth)


def shift(v, axis, s):
    n = lax.axis_size(axis)
    return lax.ppermute(v, axis, [(i, (i + s) % n) for i in range(n)])


def around(v, axis):
    return [v] + [shift(v, axis, s) for s in range(1, lax.axis_size(axis))]


def body(patch_rows, out_grads, basis_a, basis_g):
    coords = [lax.axis_index(a).astype(jnp.int32) for a in ALL]
    z = coords[3]
    x = patch_rows.transpose(0, 2, 1)
    grads = out_grads.transpose(0, 2, 1)
    here, channels = x.shape[0], x.shape[1]
    tensor = lax.axis_size("z")
    per = here // tensor

    with jax.named_scope("basis_a_x"):
        own = basis_a.reshape(AB, 3, channels, -1).transpose(0, 3, 1, 2)
        own = own.reshape(AB, own.shape[1], 3 * channels)
        ba = around(own, "x")
    with jax.named_scope("basis_g_z"):
        bg = basis_g.T
        bg = lax.all_to_all(jnp.broadcast_to(bg[None], (tensor, *bg.shape)), "z", 0, 0, tiled=True)
    with jax.named_scope("exchange_grads"):
        grads, bg, ba = lax.optimization_barrier((grads, bg, ba))
        g = lax.all_to_all(grads, "z", 0, 0, tiled=True)
    with jax.named_scope("basis_a_y"):
        ba = jnp.concatenate(ba, axis=1)
        bg, give, _ = lax.optimization_barrier((bg, x, ba))
        x_oth = shift(give, "core", 1)
        ba = around(ba, "y")
    with jax.named_scope("basis_g_x"):
        bg = around(jnp.concatenate(list(bg), axis=1), "x")

    ba, bg = lax.optimization_barrier((ba, bg))
    with jax.named_scope("basis_g_y"):
        bg = around(jnp.stack(bg), "y")
    with jax.named_scope("coeff_parts"):
        bf16 = jnp.bfloat16
        blocks = [(z + s) % tensor for s in (2, 1, 3, 0)]
        far, near = conv(jnp.stack(blocks[:2]), jnp.concatenate(ba, axis=1), x, x_oth, per, (bf16, bf16))
        received = [shift(far, "z", 2), shift(near, "z", 1)]
        ba, blocks, _ = lax.optimization_barrier((ba, blocks, far))
        last, mine = conv(jnp.stack(blocks[2:]), jnp.concatenate(ba, axis=1), x, x_oth, per, (bf16, jnp.float32))
    with jax.named_scope("exchange_cores"):
        g, bg, received, mine = lax.optimization_barrier((g, bg, received, mine))
        g_oth = shift(g, "core", 1)
        bg_oth = [shift(v, "core", 1) for v in bg]
    received.append(shift(last, "z", 3))

    examples = here * lax.axis_size(("x", "y", "core"))
    total = squares(jnp.stack(coords), mine, received, g, g_oth, bg, bg_oth, 1.0 / examples)

    with jax.named_scope("sum_examples"):
        rows = total.reshape(-1, 1, total.shape[2])
        got = lax.all_to_all(rows, ("x", "y", "z"), 0, 0, tiled=True)
        return jnp.sum(got, axis=0)


def solution(mesh):
    tensor = mesh.shape["tensor"]
    fine = Mesh(mesh.devices.reshape(4, -1, 2, tensor), ALL)
    dp = ("x", "y", "core")
    in_specs = (P(dp, None, "z"), P(dp, None, "z"), P(None, "z", dp), P("z", dp))
    return jax.shard_map(body, mesh=fine, in_specs=in_specs, out_specs=P(ALL, None), check_vma=False)
```

```python
import jax
import jax.numpy as jnp
from jax import lax
from jax.experimental import pallas as pl
from jax.experimental.pallas import tpu as pltpu
from jax.sharding import Mesh, PartitionSpec as P

SIDE = 8
POS = SIDE * SIDE * SIDE
AB = 9
ALL = ("x", "y", "core", "z")
NT = (((1,), (1,)), ((), ()))
VMEM = pl.BlockSpec(memory_space=pltpu.VMEM)
SMEM = pl.BlockSpec(memory_space=pltpu.SMEM)


def lane_coords():
    p = lax.broadcasted_iota(jnp.int32, (1, POS), 1)
    return p // 64, (p // 8) % 8, p % 8


def shifted(y, ab, i, j):
    a, b = ab // 3 - 1, ab % 3 - 1
    s = a * 64 + b * 8
    if s == 0:
        return y
    ok = None
    for v, o in ((i, a), (j, b)):
        if o != 0:
            m = (v + o >= 0) & (v + o < SIDE)
            ok = m if ok is None else ok & m
    return jnp.where(ok, pltpu.roll(y, (-s) % POS, 1), 0.0)


def conv_kernel(idx_ref, b_ref, x_ref, x_oth_ref, *refs):
    *o_refs, xc_ref = refs
    i, j, k = lane_coords()
    h = x_ref.shape[1]
    per = o_refs[0].shape[0] // 2
    ranks = b_ref.shape[1]
    zero = jnp.zeros((), x_ref.dtype)
    b = b_ref[...].reshape(AB * ranks, 3 * h)
    for n in range(2 * per * len(o_refs)):
        o, m = n // (2 * per), n % (2 * per)
        x = (x_ref if m < per else x_oth_ref)[idx_ref[o] * per + m % per]
        xc_ref[n % 2, :h] = jnp.where(k >= 1, pltpu.roll(x, 1, 1), zero)
        xc_ref[n % 2, h : 2 * h] = x
        xc_ref[n % 2, 2 * h :] = jnp.where(k <= SIDE - 2, pltpu.roll(x, POS - 1, 1), zero)
        y = jnp.dot(b, xc_ref[n % 2], preferred_element_type=jnp.float32)
        acc = None
        for ab in range(AB):
            t = shifted(y[ab * ranks : (ab + 1) * ranks], ab, i, j)
            acc = t if acc is None else acc + t
        o_refs[o][m] = acc.astype(o_refs[o].dtype)


def conv(idx, taps, x, x_oth, per, dtypes):
    ranks = taps.shape[1]
    return pl.pallas_call(
        conv_kernel,
        out_shape=[jax.ShapeDtypeStruct((2 * per, ranks, POS), d) for d in dtypes],
        in_specs=[SMEM] + [VMEM] * 3,
        out_specs=[VMEM] * len(dtypes),
        scratch_shapes=[pltpu.VMEM((2, 3 * x.shape[1], POS), jnp.bfloat16)],
        compiler_params=pltpu.CompilerParams(vmem_limit_bytes=52 << 20),
        name="conv_taps",
    )(idx, taps, x, x_oth)


def squares_kernel(idx_ref, own_ref, r1_ref, r2_ref, r3_ref, g_ref, g_oth_ref, *refs, scale):
    *bg_refs, o_ref, hi_ref, m_ref, sq_ref = refs
    x, y, core = idx_ref[0], idx_ref[1], idx_ref[2]
    side, width = len(bg_refs) // 2, bg_refs[0].shape[1]
    examples, ranks = own_ref.shape[0], own_ref.shape[1]
    per = examples // 2
    tensor = g_ref.shape[0] // per

    def chip(rx, ry):
        return ((x + side - rx) % side) * side + (y + side - ry) % side

    low_half = lax.broadcasted_iota(jnp.int32, (1, 2 * ranks), 1) < ranks
    pair = None
    for n in range(examples):
        c = own_ref[n]
        for r in (r1_ref, r2_ref, r3_ref):
            c = c + r[n].astype(jnp.float32)
        hi_ref[n] = c.astype(jnp.bfloat16)
        hi = hi_ref[n]
        lo = (c - hi.astype(jnp.float32)).astype(jnp.bfloat16)
        both = jnp.concatenate([hi, lo], axis=0)
        src = g_ref if n < per else g_oth_ref
        g = jnp.concatenate([src[t * per + n % per] for t in range(tensor)], axis=0)
        m = lax.dot_general(g, both, NT, preferred_element_type=jnp.float32)
        m = m + pltpu.roll(m, ranks, 1)
        if n % 2 == 0:
            pair = m
        else:
            m_ref[:, (n - 1) * ranks : (n + 1) * ranks] = jnp.where(low_half, pair, m).astype(jnp.bfloat16)
    m = m_ref[...]
    for half in range(2):
        for ry in range(side):
            bg = bg_refs[half * side + ry][...].reshape(side * width, -1)
            p = jnp.dot(bg, m, preferred_element_type=jnp.float32)
            p = p * p
            while p.shape[1] > 2 * ranks:
                p = p[:, : p.shape[1] // 2] + p[:, p.shape[1] // 2 :]
            p = (p + pltpu.roll(p, ranks, 1)) * scale
            for rx in range(side):
                at = (chip(rx, ry) * 2 + (core + half) % 2) * width
                sq_ref[pl.ds(pl.multiple_of(at, 8), width), :] = p[rx * width : (rx + 1) * width]
    sq = sq_ref[...].T[:ranks]
    low = ranks // (side * side)
    for b in range(side * side):
        o_ref[chip(b % side, b // side)] = sq[b * low : (b + 1) * low]


def squares(idx, own, received, g, g_oth, bg, bg_oth, scale):
    examples, ranks = own.shape[0], own.shape[1]
    side, width, hidden = bg[0].shape
    chips = side * side

    def kernel(*refs):
        squares_kernel(*refs, scale=scale)

    return pl.pallas_call(
        kernel,
        out_shape=jax.ShapeDtypeStruct((chips, ranks // chips, 2 * chips * width), jnp.float32),
        in_specs=[SMEM] + [VMEM] * (6 + 2 * side),
        out_specs=VMEM,
        scratch_shapes=[
            pltpu.VMEM((examples, ranks, POS), jnp.bfloat16),
            pltpu.VMEM((hidden, examples * ranks), jnp.bfloat16),
            pltpu.VMEM((2 * chips * width, 2 * ranks), jnp.float32),
        ],
        compiler_params=pltpu.CompilerParams(vmem_limit_bytes=52 << 20),
        name="squared_sums",
    )(idx, own, *received, g, g_oth, *bg, *bg_oth)


def shift(v, axis, s):
    n = lax.axis_size(axis)
    return lax.ppermute(v, axis, [(i, (i + s) % n) for i in range(n)])


def around(v, axis):
    return [v] + [shift(v, axis, s) for s in range(1, lax.axis_size(axis))]


def body(patch_rows, out_grads, basis_a, basis_g):
    coords = [lax.axis_index(a).astype(jnp.int32) for a in ALL]
    z = coords[3]
    x = patch_rows.transpose(0, 2, 1)
    grads = out_grads.transpose(0, 2, 1)
    here, channels = x.shape[0], x.shape[1]
    tensor = lax.axis_size("z")
    per = here // tensor

    with jax.named_scope("basis_a_x"):
        own = basis_a.reshape(AB, 3, channels, -1).transpose(0, 3, 1, 2)
        own = own.reshape(AB, own.shape[1], 3 * channels)
        ba = around(own, "x")
    with jax.named_scope("basis_g_z"):
        bg = basis_g.T
        bg = lax.all_to_all(jnp.broadcast_to(bg[None], (tensor, *bg.shape)), "z", 0, 0, tiled=True)
    with jax.named_scope("exchange_grads"):
        grads, bg, ba = lax.optimization_barrier((grads, bg, ba))
        g = lax.all_to_all(grads, "z", 0, 0, tiled=True)
    with jax.named_scope("basis_a_y"):
        ba = jnp.concatenate(ba, axis=1)
        bg, give, _ = lax.optimization_barrier((bg, x, ba))
        x_oth = shift(give, "core", 1)
        ba = around(ba, "y")
    with jax.named_scope("basis_g_x"):
        bg = around(jnp.concatenate(list(bg), axis=1), "x")

    ba, bg = lax.optimization_barrier((ba, bg))
    with jax.named_scope("basis_g_y"):
        bg = around(jnp.stack(bg), "y")
    with jax.named_scope("coeff_parts"):
        bf16 = jnp.bfloat16
        blocks = [(z + s) % tensor for s in (2, 1, 3, 0)]
        near, far = conv(jnp.stack(blocks[1::-1]), jnp.concatenate(ba, axis=1), x, x_oth, per, (bf16, bf16))
        received = [shift(far, "z", 2), shift(near, "z", 1)]
        ba, blocks, _ = lax.optimization_barrier((ba, blocks, far))
        (last,) = conv(blocks[2].reshape(1), jnp.concatenate(ba, axis=1), x, x_oth, per, (bf16,))
        received.append(shift(last, "z", 3))
        ba, blocks, _ = lax.optimization_barrier((ba, blocks, last))
        (mine,) = conv(blocks[3].reshape(1), jnp.concatenate(ba, axis=1), x, x_oth, per, (jnp.float32,))
    with jax.named_scope("exchange_cores"):
        g, bg, received, mine = lax.optimization_barrier((g, bg, received, mine))
        g_oth = shift(g, "core", 1)
        bg_oth = [shift(v, "core", 1) for v in bg]

    examples = here * lax.axis_size(("x", "y", "core"))
    total = squares(jnp.stack(coords), mine, received, g, g_oth, bg, bg_oth, 1.0 / examples)

    with jax.named_scope("sum_examples"):
        rows = total.reshape(-1, 1, total.shape[2])
        got = lax.all_to_all(rows, ("x", "y", "z"), 0, 0, tiled=True)
        return jnp.sum(got, axis=0)


def solution(mesh):
    tensor = mesh.shape["tensor"]
    fine = Mesh(mesh.devices.reshape(4, -1, 2, tensor), ALL)
    dp = ("x", "y", "core")
    in_specs = (P(dp, None, "z"), P(dp, None, "z"), P(None, "z", dp), P("z", dp))
    return jax.shard_map(body, mesh=fine, in_specs=in_specs, out_specs=P(ALL, None), check_vma=False)
```

```python
import jax
import jax.numpy as jnp
from jax import lax
from jax.experimental import pallas as pl
from jax.experimental.pallas import tpu as pltpu
from jax.sharding import Mesh, PartitionSpec as P

SIDE = 8
POS = SIDE * SIDE * SIDE
AB = 9
ALL = ("x", "y", "core", "z")
NT = (((1,), (1,)), ((), ()))
VMEM = pl.BlockSpec(memory_space=pltpu.VMEM)
SMEM = pl.BlockSpec(memory_space=pltpu.SMEM)


def lane_coords():
    p = lax.broadcasted_iota(jnp.int32, (1, POS), 1)
    return p // 64, (p // 8) % 8, p % 8


def shifted(y, ab, i, j):
    a, b = ab // 3 - 1, ab % 3 - 1
    s = a * 64 + b * 8
    if s == 0:
        return y
    ok = None
    for v, o in ((i, a), (j, b)):
        if o != 0:
            m = (v + o >= 0) & (v + o < SIDE)
            ok = m if ok is None else ok & m
    return jnp.where(ok, pltpu.roll(y, (-s) % POS, 1), 0.0)


def conv_kernel(idx_ref, b_ref, x_ref, x_oth_ref, *refs):
    *o_refs, xc_ref = refs
    i, j, k = lane_coords()
    h = x_ref.shape[1]
    per = o_refs[0].shape[0] // 2
    ranks = b_ref.shape[1]
    zero = jnp.zeros((), x_ref.dtype)
    b = b_ref[...].reshape(AB * ranks, 3 * h)
    for n in range(2 * per * len(o_refs)):
        o, m = n // (2 * per), n % (2 * per)
        x = (x_ref if m < per else x_oth_ref)[idx_ref[o] * per + m % per]
        xc_ref[n % 2, :h] = jnp.where(k >= 1, pltpu.roll(x, 1, 1), zero)
        xc_ref[n % 2, h : 2 * h] = x
        xc_ref[n % 2, 2 * h :] = jnp.where(k <= SIDE - 2, pltpu.roll(x, POS - 1, 1), zero)
        y = jnp.dot(b, xc_ref[n % 2], preferred_element_type=jnp.float32)
        acc = None
        for ab in range(AB):
            t = shifted(y[ab * ranks : (ab + 1) * ranks], ab, i, j)
            acc = t if acc is None else acc + t
        o_refs[o][m] = acc.astype(o_refs[o].dtype)


def conv(idx, taps, x, x_oth, per, dtypes):
    ranks = taps.shape[1]
    return pl.pallas_call(
        conv_kernel,
        out_shape=[jax.ShapeDtypeStruct((2 * per, ranks, POS), d) for d in dtypes],
        in_specs=[SMEM] + [VMEM] * 3,
        out_specs=[VMEM] * len(dtypes),
        scratch_shapes=[pltpu.VMEM((2, 3 * x.shape[1], POS), jnp.bfloat16)],
        compiler_params=pltpu.CompilerParams(vmem_limit_bytes=52 << 20),
        name="conv_taps",
    )(idx, taps, x, x_oth)


def squares_kernel(idx_ref, own_ref, r1_ref, r2_ref, r3_ref, g_ref, g_oth_ref, *refs, scale):
    *bg_refs, o_ref, hi_ref, m_ref, sq_ref = refs
    x, y, core = idx_ref[0], idx_ref[1], idx_ref[2]
    side, width = len(bg_refs) // 2, bg_refs[0].shape[1]
    examples, ranks = own_ref.shape[0], own_ref.shape[1]
    per = examples // 2
    tensor = g_ref.shape[0] // per

    def chip(rx, ry):
        return ((x + side - rx) % side) * side + (y + side - ry) % side

    low_half = lax.broadcasted_iota(jnp.int32, (1, 2 * ranks), 1) < ranks
    pair = None
    for n in range(examples):
        c = own_ref[n]
        for r in (r1_ref, r2_ref, r3_ref):
            c = c + r[n].astype(jnp.float32)
        hi_ref[n] = c.astype(jnp.bfloat16)
        hi = hi_ref[n]
        lo = (c - hi.astype(jnp.float32)).astype(jnp.bfloat16)
        both = jnp.concatenate([hi, lo], axis=0)
        src = g_ref if n < per else g_oth_ref
        g = jnp.concatenate([src[t * per + n % per] for t in range(tensor)], axis=0)
        m = lax.dot_general(g, both, NT, preferred_element_type=jnp.float32)
        m = m + pltpu.roll(m, ranks, 1)
        if n % 2 == 0:
            pair = m
        else:
            m_ref[:, (n - 1) * ranks : (n + 1) * ranks] = jnp.where(low_half, pair, m).astype(jnp.bfloat16)
    m = m_ref[...]
    for half in range(2):
        for ry in range(side):
            bg = bg_refs[half * side + ry][...].reshape(side * width, -1)
            p = jnp.dot(bg, m, preferred_element_type=jnp.float32)
            p = p * p
            while p.shape[1] > 2 * ranks:
                p = p[:, : p.shape[1] // 2] + p[:, p.shape[1] // 2 :]
            p = (p + pltpu.roll(p, ranks, 1)) * scale
            for rx in range(side):
                at = (chip(rx, ry) * 2 + (core + half) % 2) * width
                sq_ref[pl.ds(pl.multiple_of(at, 8), width), :] = p[rx * width : (rx + 1) * width]
    sq = sq_ref[...].T[:ranks]
    low = ranks // (side * side)
    for b in range(side * side):
        o_ref[chip(b % side, b // side)] = sq[b * low : (b + 1) * low]


def squares(idx, own, received, g, g_oth, bg, bg_oth, scale):
    examples, ranks = own.shape[0], own.shape[1]
    side, width, hidden = bg[0].shape
    chips = side * side

    def kernel(*refs):
        squares_kernel(*refs, scale=scale)

    return pl.pallas_call(
        kernel,
        out_shape=jax.ShapeDtypeStruct((chips, ranks // chips, 2 * chips * width), jnp.float32),
        in_specs=[SMEM] + [VMEM] * (6 + 2 * side),
        out_specs=VMEM,
        scratch_shapes=[
            pltpu.VMEM((examples, ranks, POS), jnp.bfloat16),
            pltpu.VMEM((hidden, examples * ranks), jnp.bfloat16),
            pltpu.VMEM((2 * chips * width, 2 * ranks), jnp.float32),
        ],
        compiler_params=pltpu.CompilerParams(vmem_limit_bytes=52 << 20),
        name="squared_sums",
    )(idx, own, *received, g, g_oth, *bg, *bg_oth)


def shift(v, axis, s):
    n = lax.axis_size(axis)
    return lax.ppermute(v, axis, [(i, (i + s) % n) for i in range(n)])


def around(v, axis):
    return [v] + [shift(v, axis, s) for s in range(1, lax.axis_size(axis))]


def body(patch_rows, out_grads, basis_a, basis_g):
    coords = [lax.axis_index(a).astype(jnp.int32) for a in ALL]
    z = coords[3]
    x = patch_rows.transpose(0, 2, 1)
    grads = out_grads.transpose(0, 2, 1)
    here, channels = x.shape[0], x.shape[1]
    tensor = lax.axis_size("z")
    per = here // tensor

    with jax.named_scope("basis_a_x"):
        own = basis_a.reshape(AB, 3, channels, -1).transpose(0, 3, 1, 2)
        own = own.reshape(AB, own.shape[1], 3 * channels)
        ba = around(own, "x")
    with jax.named_scope("basis_g_z"):
        bg = basis_g.T
        bg = lax.all_to_all(jnp.broadcast_to(bg[None], (tensor, *bg.shape)), "z", 0, 0, tiled=True)
    with jax.named_scope("exchange_grads"):
        grads, bg, ba = lax.optimization_barrier((grads, bg, ba))
        g = lax.all_to_all(grads, "z", 0, 0, tiled=True)
    with jax.named_scope("basis_a_y"):
        ba = jnp.concatenate(ba, axis=1)
        bg, give, _ = lax.optimization_barrier((bg, x, ba))
        x_oth = shift(give, "core", 1)
        ba = around(ba, "y")
    with jax.named_scope("basis_g_x"):
        bg = around(jnp.concatenate(list(bg), axis=1), "x")

    ba, bg = lax.optimization_barrier((ba, bg))
    with jax.named_scope("basis_g_y"):
        bg = around(jnp.stack(bg), "y")
    with jax.named_scope("coeff_parts"):
        bf16 = jnp.bfloat16
        blocks = [(z + s) % tensor for s in (2, 1, 3, 0)]
        far, near = conv(jnp.stack(blocks[:2]), jnp.concatenate(ba, axis=1), x, x_oth, per, (bf16, bf16))
        received = [shift(far, "z", 2), shift(near, "z", 1)]
        ba, blocks, _ = lax.optimization_barrier((ba, blocks, far))
        last, mine = conv(jnp.stack(blocks[2:]), jnp.concatenate(ba, axis=1), x, x_oth, per, (bf16, jnp.float32))
    with jax.named_scope("exchange_cores"):
        g, bg, received[0], last = lax.optimization_barrier((g, bg, received[0], last))
        g_oth = shift(g, "core", 1)
        bg_oth = [shift(v, "core", 1) for v in bg]
    received.append(shift(last, "z", 3))

    examples = here * lax.axis_size(("x", "y", "core"))
    total = squares(jnp.stack(coords), mine, received, g, g_oth, bg, bg_oth, 1.0 / examples)

    with jax.named_scope("sum_examples"):
        rows = total.reshape(-1, 1, total.shape[2])
        got = lax.all_to_all(rows, ("x", "y", "z"), 0, 0, tiled=True)
        return jnp.sum(got, axis=0)


def solution(mesh):
    tensor = mesh.shape["tensor"]
    fine = Mesh(mesh.devices.reshape(4, -1, 2, tensor), ALL)
    dp = ("x", "y", "core")
    in_specs = (P(dp, None, "z"), P(dp, None, "z"), P(None, "z", dp), P("z", dp))
    return jax.shard_map(body, mesh=fine, in_specs=in_specs, out_specs=P(ALL, None), check_vma=False)
```

```python
import jax
import jax.numpy as jnp
from jax import lax
from jax.experimental import pallas as pl
from jax.experimental.pallas import tpu as pltpu
from jax.sharding import Mesh, PartitionSpec as P

SIDE = 8
POS = SIDE * SIDE * SIDE
AB = 9
ALL = ("x", "y", "core", "z")
NT = (((1,), (1,)), ((), ()))
VMEM = pl.BlockSpec(memory_space=pltpu.VMEM)
SMEM = pl.BlockSpec(memory_space=pltpu.SMEM)


def lane_coords():
    p = lax.broadcasted_iota(jnp.int32, (1, POS), 1)
    return p // 64, (p // 8) % 8, p % 8


def shifted(y, ab, i, j):
    a, b = ab // 3 - 1, ab % 3 - 1
    s = a * 64 + b * 8
    if s == 0:
        return y
    ok = None
    for v, o in ((i, a), (j, b)):
        if o != 0:
            m = (v + o >= 0) & (v + o < SIDE)
            ok = m if ok is None else ok & m
    return jnp.where(ok, pltpu.roll(y, (-s) % POS, 1), 0.0)


def conv_kernel(idx_ref, b_ref, x_ref, x_oth_ref, *refs):
    *o_refs, xc_ref = refs
    i, j, k = lane_coords()
    h = x_ref.shape[1]
    per = o_refs[0].shape[0] // 2
    ranks = b_ref.shape[1]
    zero = jnp.zeros((), x_ref.dtype)
    b = b_ref[...].reshape(AB * ranks, 3 * h)
    for n in range(2 * per * len(o_refs)):
        o, m = n // (2 * per), n % (2 * per)
        x = (x_ref if m < per else x_oth_ref)[idx_ref[o] * per + m % per]
        xc_ref[n % 2, :h] = jnp.where(k >= 1, pltpu.roll(x, 1, 1), zero)
        xc_ref[n % 2, h : 2 * h] = x
        xc_ref[n % 2, 2 * h :] = jnp.where(k <= SIDE - 2, pltpu.roll(x, POS - 1, 1), zero)
        y = jnp.dot(b, xc_ref[n % 2], preferred_element_type=jnp.float32)
        acc = None
        for ab in range(AB):
            t = shifted(y[ab * ranks : (ab + 1) * ranks], ab, i, j)
            acc = t if acc is None else acc + t
        o_refs[o][m] = acc.astype(o_refs[o].dtype)


def conv(idx, taps, x, x_oth, per, dtypes):
    ranks = taps.shape[1]
    return pl.pallas_call(
        conv_kernel,
        out_shape=[jax.ShapeDtypeStruct((2 * per, ranks, POS), d) for d in dtypes],
        in_specs=[SMEM] + [VMEM] * 3,
        out_specs=[VMEM] * len(dtypes),
        scratch_shapes=[pltpu.VMEM((2, 3 * x.shape[1], POS), jnp.bfloat16)],
        compiler_params=pltpu.CompilerParams(vmem_limit_bytes=52 << 20),
        name="conv_taps",
    )(idx, taps, x, x_oth)


def squares_kernel(idx_ref, own_ref, r1_ref, r2_ref, r3_ref, g_ref, g_oth_ref, *refs, scale):
    *bg_refs, o_ref, hi_ref, m_ref, sq_ref = refs
    x, y, core = idx_ref[0], idx_ref[1], idx_ref[2]
    side, width = len(bg_refs) // 2, bg_refs[0].shape[1]
    examples, ranks = own_ref.shape[0], own_ref.shape[1]
    per = examples // 2
    tensor = g_ref.shape[0] // per

    def chip(rx, ry):
        return ((x + side - rx) % side) * side + (y + side - ry) % side

    low_half = lax.broadcasted_iota(jnp.int32, (1, 2 * ranks), 1) < ranks
    pair = None
    for n in range(examples):
        c = own_ref[n]
        for r in (r1_ref, r2_ref, r3_ref):
            c = c + r[n].astype(jnp.float32)
        hi_ref[n] = c.astype(jnp.bfloat16)
        hi = hi_ref[n]
        lo = (c - hi.astype(jnp.float32)).astype(jnp.bfloat16)
        both = jnp.concatenate([hi, lo], axis=0)
        src = g_ref if n < per else g_oth_ref
        g = jnp.concatenate([src[t * per + n % per] for t in range(tensor)], axis=0)
        m = lax.dot_general(g, both, NT, preferred_element_type=jnp.float32)
        m = m + pltpu.roll(m, ranks, 1)
        if n % 2 == 0:
            pair = m
        else:
            m_ref[:, (n - 1) * ranks : (n + 1) * ranks] = jnp.where(low_half, pair, m).astype(jnp.bfloat16)
    m = m_ref[...]
    for half in range(2):
        for ry in range(side):
            bg = bg_refs[half * side + ry][...].reshape(side * width, -1)
            p = jnp.dot(bg, m, preferred_element_type=jnp.float32)
            p = p * p
            while p.shape[1] > 2 * ranks:
                p = p[:, : p.shape[1] // 2] + p[:, p.shape[1] // 2 :]
            p = (p + pltpu.roll(p, ranks, 1)) * scale
            for rx in range(side):
                at = (chip(rx, ry) * 2 + (core + half) % 2) * width
                sq_ref[pl.ds(pl.multiple_of(at, 8), width), :] = p[rx * width : (rx + 1) * width]
    sq = sq_ref[...].T[:ranks]
    low = ranks // (side * side)
    for b in range(side * side):
        o_ref[chip(b % side, b // side)] = sq[b * low : (b + 1) * low]


def squares(idx, own, received, g, g_oth, bg, bg_oth, scale):
    examples, ranks = own.shape[0], own.shape[1]
    side, width, hidden = bg[0].shape
    chips = side * side

    def kernel(*refs):
        squares_kernel(*refs, scale=scale)

    return pl.pallas_call(
        kernel,
        out_shape=jax.ShapeDtypeStruct((chips, ranks // chips, 2 * chips * width), jnp.float32),
        in_specs=[SMEM] + [VMEM] * (6 + 2 * side),
        out_specs=VMEM,
        scratch_shapes=[
            pltpu.VMEM((examples, ranks, POS), jnp.bfloat16),
            pltpu.VMEM((hidden, examples * ranks), jnp.bfloat16),
            pltpu.VMEM((2 * chips * width, 2 * ranks), jnp.float32),
        ],
        compiler_params=pltpu.CompilerParams(vmem_limit_bytes=52 << 20),
        name="squared_sums",
    )(idx, own, *received, g, g_oth, *bg, *bg_oth)


def shift(v, axis, s):
    n = lax.axis_size(axis)
    return lax.ppermute(v, axis, [(i, (i + s) % n) for i in range(n)])


def around(v, axis):
    return [v] + [shift(v, axis, s) for s in range(1, lax.axis_size(axis))]


def body(patch_rows, out_grads, basis_a, basis_g):
    coords = [lax.axis_index(a).astype(jnp.int32) for a in ALL]
    z = coords[3]
    x = patch_rows.transpose(0, 2, 1)
    grads = out_grads.transpose(0, 2, 1)
    here, channels = x.shape[0], x.shape[1]
    tensor = lax.axis_size("z")
    per = here // tensor

    with jax.named_scope("basis_a_x"):
        own = basis_a.reshape(AB, 3, channels, -1).transpose(0, 3, 1, 2)
        own = own.reshape(AB, own.shape[1], 3 * channels)
        ba = around(own, "x")
    with jax.named_scope("basis_g_z"):
        bg = basis_g.T
        bg = lax.all_to_all(jnp.broadcast_to(bg[None], (tensor, *bg.shape)), "z", 0, 0, tiled=True)
    with jax.named_scope("exchange_grads"):
        grads, bg, ba = lax.optimization_barrier((grads, bg, ba))
        g = lax.all_to_all(grads, "z", 0, 0, tiled=True)
    with jax.named_scope("basis_a_y"):
        ba = jnp.concatenate(ba, axis=1)
        bg, give, _ = lax.optimization_barrier((bg, x, ba))
        x_oth = shift(give, "core", 1)
        ba = around(ba, "y")
    with jax.named_scope("basis_g_x"):
        bg = around(jnp.concatenate(list(bg), axis=1), "x")

    ba, bg = lax.optimization_barrier((ba, bg))
    with jax.named_scope("basis_g_y"):
        bg = around(jnp.stack(bg), "y")
    with jax.named_scope("coeff_parts"):
        bf16 = jnp.bfloat16
        blocks = [(z + s) % tensor for s in (2, 1, 3, 0)]
        far, near = conv(jnp.stack(blocks[:2]), jnp.concatenate(ba, axis=1), x, x_oth, per, (bf16, bf16))
        received = [shift(far, "z", 2), shift(near, "z", 1)]
        ba, blocks, _ = lax.optimization_barrier((ba, blocks, far))
        last, mine = conv(jnp.stack(blocks[2:]), jnp.concatenate(ba, axis=1), x, x_oth, per, (bf16, jnp.float32))
    with jax.named_scope("exchange_cores"):
        g, bg, received[0], last = lax.optimization_barrier((g, bg, received[0], last))
        g_oth = shift(g, "core", 1)
        bg_oth = [shift(v, "core", 1) for v in bg]
    received.append(shift(last, "z", 3))

    examples = here * lax.axis_size(("x", "y", "core"))
    total = squares(jnp.stack(coords), mine, received, g, g_oth, bg, bg_oth, 1.0 / examples)

    with jax.named_scope("sum_examples"):
        rows = total.reshape(-1, 1, total.shape[2]).astype(jnp.bfloat16)
        got = lax.all_to_all(rows, ("x", "y", "z"), 0, 0, tiled=True)
        return jnp.sum(got.astype(jnp.float32), axis=0)


def solution(mesh):
    tensor = mesh.shape["tensor"]
    fine = Mesh(mesh.devices.reshape(4, -1, 2, tensor), ALL)
    dp = ("x", "y", "core")
    in_specs = (P(dp, None, "z"), P(dp, None, "z"), P(None, "z", dp), P("z", dp))
    return jax.shard_map(body, mesh=fine, in_specs=in_specs, out_specs=P(ALL, None), check_vma=False)
```
